256 devices in a mesh: tp: 16 (over x_lo, y, core), grp: 16 (over z, x_hi).
Axes of the slice: x: 4 (x_hi: 2, x_lo: 2; x = x_hi * 2 + x_lo), y: 4, z: 8, core: 2. Of those that a mesh axis runs over, the one named last changes fastest.
Arguments:
- resid_in: bfloat16 [1024, 8192], P('grp', 'tp'), may hold values from -6 to 6
- queries: bfloat16 [1024, 4096], P('grp', 'tp')
- kv_cache: bfloat16 [2, 1024, 16, 128, 128], P(None, 'grp', 'tp'), as said below
- new_kv: bfloat16 [2, 1024, 4, 128], P(None, 'grp')
- lengths: int32 [1024], P('grp'), may hold values from 1 to 128, 65536 in all
- out_weight: bfloat16 [4096, 8192], P('tp'), may hold values from -0.09375 to 0.09375
- enc_weight: bfloat16 [8192, 32768], P('tp', 'grp'), may hold values from -0.0625 to 0.0625
- enc_bias: float32 [32768], P('grp'), may hold values from -1 to 0.5
- dec_weight: bfloat16 [32768, 8192], P('grp', 'tp'), may hold values from -0.75 to 0.75
- clamp_ids: int32 [1024, 4], P('grp'), may hold values from 0 to 32767, as said below
- clamp_values: float32 [1024, 4], P('grp'), may hold values from 2 to 8
Outputs:
- resid_out: bfloat16 [1024, 8192], P('grp', 'tp')
- features: bfloat16 [1024, 32768], P('tp', 'grp')
The draws below stay inside these ranges and needn't reach their ends.
Inputs may be any that keep to these rules, and one draw needn't show every extreme that they name: Entries of kv_cache whose third index divided by 4 agrees are equal. `clamp_ids`: a row's 4 ids are (b + c * 8192) modulo 32768 for c = 0 .. 3.
All inputs are finite; a program needn't handle non-finite values. No bound on the sum of `lengths` on one device may be relied on, other than what follows from the above.
Results may differ from the reference program's by a relative error of at most 0.008.
Values may be sent and summed in bfloat16 or wider, within the bound.
No kernel may reach another device: no remote copies, remote signals or barrier semaphores. Data moves between devices by JAX's collectives and lax.ppermute only.
A program may use at most 128 MiB of HBM per device.

```python
import math
import jax
import jax.numpy as jnp
import numpy as np
from jax import lax

D = 8192
HEAD_DIM = 128
HEADS = 32
KV_HEADS = 4
LATENTS = 32768
CLAMPS = 4
CACHE_LEN = 128
SEQS = 1024
KV_COPIES = 16


def draw_queries(key, part):
    group_size = HEADS // KV_HEADS
    shape = (SEQS, KV_HEADS, group_size, HEAD_DIM)
    base = jnp.clip(jax.random.normal(jax.random.fold_in(key, 11), shape, jnp.float32), -6.0, 6.0)
    return base.reshape(SEQS, HEADS * HEAD_DIM).astype(jnp.bfloat16)


def draw_kv_cache(key, part):
    shape = (2, SEQS, KV_HEADS, CACHE_LEN, HEAD_DIM)
    base = jnp.clip(jax.random.normal(jax.random.fold_in(key, 12), shape, jnp.float32), -6.0, 6.0)
    return jnp.repeat(base, KV_COPIES // KV_HEADS, axis=2).astype(jnp.bfloat16)


def draw_new_kv(key, part):
    shape = (2, SEQS, KV_HEADS, HEAD_DIM)
    base = jnp.clip(jax.random.normal(jax.random.fold_in(key, 13), shape, jnp.float32), -6.0, 6.0)
    return base.astype(jnp.bfloat16)


def draw_clamp_ids(key, part):
    first_id = jax.random.randint(jax.random.fold_in(key, 5), (SEQS, 1), 0, LATENTS, dtype=jnp.int32)
    row_index = jnp.arange(SEQS, dtype=jnp.int32)[:, None]
    first_id = jnp.where(row_index == 0, LATENTS - 1, first_id)
    first_id = jnp.where(row_index == 1, 0, first_id)
    spacing = jnp.arange(CLAMPS, dtype=jnp.int32)[None, :] * (LATENTS // CLAMPS)
    return ((first_id + spacing) % LATENTS).astype(jnp.int32)


def levels(rng, extent, split, least, high):
    gain = 1.0
    for position, blocks in split:
        steps = jax.random.uniform(jax.random.fold_in(jax.random.fold_in(rng, 6), position), (blocks,), jnp.float32, least / len(split), high / len(split))
        gain = gain * jnp.repeat(jnp.exp(steps), extent[position] // blocks).reshape((-1,) + (1,) * (len(extent) - 1 - position))
    return gain


def split_up(number_of, total, reach, lean):
    weights = [(1 << 20) // math.isqrt(grade ** lean) + 1 for grade in range(2, number_of + 1)]
    spare, given = total - reach - (number_of - 1), [1] * (number_of - 1)
    while spare > 0:
        movable = [i for i in range(number_of - 1) if given[i] < reach]
        pool, left = sum([weights[i] for i in movable]), spare
        for i in movable:
            more = min(reach - given[i], max(1, left * weights[i] // pool), spare)
            given[i] = given[i] + more
            spare = spare - more
    return np.array([reach] + given)


def ragged_sizes(key, number_of, total, most, slope):
    if number_of == 2:
        one = jax.random.randint(key, (), max(1, total - most), min(most, total - 1) + 1)
        return jnp.stack([one, total - one])
    sizes = jnp.asarray(split_up(number_of, total, most, slope), jnp.int32)
    couples = (number_of - 1) // 2
    donor, taker = sizes[1:1 + 2 * couples:2], sizes[2:2 + 2 * couples:2]
    margin = jnp.minimum(donor - 1, most - taker)
    shifted = jax.random.randint(jax.random.fold_in(key, 1), (couples,), 0, 1 << 20) % (margin + 1)
    sizes = sizes.at[1:1 + 2 * couples:2].set(donor - shifted).at[2:2 + 2 * couples:2].set(taker + shifted)
    return sizes[jax.random.permutation(jax.random.fold_in(key, 2), number_of)]


def centred(key, extent, spread, bound, pieces=(), kind=jnp.bfloat16):
    values = spread * jax.random.normal(key, extent, jnp.float32)
    if pieces:
        values = values * levels(key, extent, pieces, -0.22, 0.18)
    return jnp.clip(values, -bound, bound).astype(kind)


def setup_inputs(seed: int = 0) -> dict:
    arg_keys = jax.random.split(jax.random.key(seed), 12)
    return {
        "resid_in": centred(arg_keys[0], (SEQS, D), 1.0, 6.0, ((0, 16), (1, 16))),
        "queries": draw_queries(jax.random.fold_in(arg_keys[11], 71), 0),
        "kv_cache": draw_kv_cache(jax.random.fold_in(arg_keys[11], 71), 0),
        "new_kv": draw_new_kv(jax.random.fold_in(arg_keys[11], 71), 0),
        "lengths": ragged_sizes(arg_keys[4], SEQS, SEQS * CACHE_LEN // 2, CACHE_LEN, 2).astype(jnp.int32),
        "out_weight": centred(arg_keys[5], (HEADS * HEAD_DIM, D), (HEADS * HEAD_DIM) ** -0.5, 0.09375, ((0, 16),)),
        "enc_weight": centred(arg_keys[6], (D, LATENTS), D ** -0.5, 0.0625, ((0, 16), (1, 16))),
        "enc_bias": jnp.clip(-1.0 + 1.5 * jax.random.uniform(arg_keys[7], (LATENTS,), jnp.float32) ** levels(arg_keys[7], (LATENTS,), ((0, 16),), -0.2, 0.2), -1.0, 0.5),
        "dec_weight": centred(arg_keys[8], (LATENTS, D), 64 ** -0.5, 0.75, ((0, 16), (1, 16))),
        "clamp_ids": draw_clamp_ids(jax.random.fold_in(arg_keys[11], 71), 0),
        "clamp_values": jnp.clip(2.0 + 6.0 * jax.random.uniform(arg_keys[10], (SEQS, CLAMPS), jnp.float32) ** levels(arg_keys[10], (SEQS, CLAMPS), ((0, 16),), -0.2, 0.2), 2.0, 8.0),
    }


def reference(resid_in, queries, kv_cache, new_kv, lengths, out_weight, enc_weight, enc_bias, dec_weight, clamp_ids, clamp_values):
    group_size = HEADS // KV_HEADS
    score_scale = HEAD_DIM ** -0.5
    cache_view = kv_cache[:, :, ::(KV_COPIES // KV_HEADS)]
    query_heads = queries.astype(jnp.float32).reshape(SEQS, KV_HEADS, group_size, HEAD_DIM)
    cache_keys = cache_view[0].astype(jnp.float32)
    cache_values = cache_view[1].astype(jnp.float32)
    scores = jnp.einsum("skgd,skpd->skgp", query_heads, cache_keys) * score_scale
    new_score = jnp.einsum("skgd,skd->skg", query_heads, new_kv[0].astype(jnp.float32)) * score_scale
    slot_index = jnp.arange(CACHE_LEN, dtype=jnp.int32)
    is_valid = (slot_index[None, :] < lengths[:, None])[:, None, None, :]
    top_score = jnp.maximum(jnp.max(jnp.where(is_valid, scores, -jnp.inf), axis=-1), new_score)
    prob_cache = jnp.where(is_valid, jnp.exp(scores - top_score[..., None]), 0.0)
    new_prob = jnp.exp(new_score - top_score)
    total_weight = jnp.sum(prob_cache, axis=-1) + new_prob
    cache_rounded = lax.optimization_barrier(prob_cache.astype(jnp.bfloat16)).astype(jnp.float32)
    new_rounded = lax.optimization_barrier(new_prob.astype(jnp.bfloat16)).astype(jnp.float32)
    weighted = jnp.einsum("skgp,skpd->skgd", cache_rounded, cache_values)
    weighted = weighted + new_rounded[..., None] * new_kv[1].astype(jnp.float32)[:, :, None, :]
    head_output = (weighted / total_weight[..., None]).astype(jnp.bfloat16).reshape(SEQS, HEADS * HEAD_DIM)
    attn_out = jnp.dot(head_output, out_weight, preferred_element_type=jnp.float32)
    resid_mid = (resid_in.astype(jnp.float32) + attn_out).astype(jnp.bfloat16)
    pre_act = jnp.dot(resid_mid.astype(jnp.float32), enc_weight.astype(jnp.float32))
    features = jnp.maximum(pre_act + enc_bias, 0.0).astype(jnp.bfloat16)
    clamped_now = jnp.take_along_axis(features, clamp_ids, axis=1).astype(jnp.float32)
    delta_at = (clamp_values - clamped_now).astype(jnp.bfloat16)
    decoder_rows = dec_weight[clamp_ids]
    edit_sum = jnp.einsum("sc,scd->sd", delta_at.astype(jnp.float32), decoder_rows.astype(jnp.float32))
    resid_out = (resid_mid.astype(jnp.float32) + edit_sum).astype(jnp.bfloat16)
    return resid_out, features
```

```python
import jax
import jax.numpy as jnp
from jax import lax
from jax.sharding import PartitionSpec as P

HEAD_DIM = 128
KV_HEADS = 4
CORES, CHIPS, RINGS, PLANES = 2, 8, 4, 2


def tp_moves(move):
    return [(chip * 2 + core, move(chip, core)) for chip in range(8) for core in range(2)]


def grp_moves(move):
    return [(z * 2 + plane, move(z, plane)) for z in range(8) for plane in range(2)]


def swap_core(value):
    return lax.ppermute(value, "tp", tp_moves(lambda chip, core: chip * 2 + 1 - core))


def from_z(value, ahead):
    return lax.ppermute(
        value, "grp", grp_moves(lambda z, plane: (z - ahead) % 8 * 2 + plane)
    )


def chip_at(chip, dx, dy):
    return (chip // 4 + dx) % 2 * 4 + (chip + dy) % 4


def to_chip(value, dx, dy):
    return lax.ppermute(
        value, "tp", tp_moves(lambda chip, core: chip_at(chip, dx, dy) * 2 + core)
    )


def attend(queries, kv_cache, new_kv, lengths, kv_index):
    row_count = queries.shape[0]
    own_heads = queries.shape[1] // HEAD_DIM
    slot_count = kv_cache.shape[3]
    score_scale = HEAD_DIM ** (-0.5)
    query_heads = queries.reshape(row_count, own_heads, HEAD_DIM)
    cache_keys = kv_cache[0, :, 0]
    cache_values = kv_cache[1, :, 0]
    new_key = lax.dynamic_index_in_dim(new_kv[0], kv_index, 1, keepdims=False)
    new_value = lax.dynamic_index_in_dim(new_kv[1], kv_index, 1, keepdims=False)
    scores = (
        jnp.einsum("shd,spd->shp", query_heads, cache_keys, preferred_element_type=jnp.float32)
        * score_scale
    )
    new_score = (
        jnp.einsum("shd,sd->sh", query_heads, new_key, preferred_element_type=jnp.float32)
        * score_scale
    )
    slot_index = jnp.arange(slot_count, dtype=jnp.int32)
    is_valid = (slot_index[None, :] < lengths[:, None])[:, None, :]
    top_score = jnp.maximum(jnp.max(jnp.where(is_valid, scores, -jnp.inf), axis=-1), new_score)
    prob_cache = jnp.where(is_valid, jnp.exp(scores - top_score[..., None]), 0.0)
    new_prob = jnp.exp(new_score - top_score)
    total_weight = jnp.sum(prob_cache, axis=-1) + new_prob
    new_rounded = lax.optimization_barrier(new_prob.astype(jnp.bfloat16)).astype(jnp.float32)
    weighted = jnp.einsum(
        "shp,spd->shd",
        prob_cache.astype(jnp.bfloat16),
        cache_values,
        preferred_element_type=jnp.float32,
    )
    weighted = weighted + new_rounded[..., None] * new_value.astype(jnp.float32)[:, None, :]
    return (
        (weighted / total_weight[..., None])
        .astype(jnp.bfloat16)
        .reshape(row_count, own_heads * HEAD_DIM)
    )


def mm(a, b):
    return jnp.dot(a, b, preferred_element_type=jnp.float32)


def per_device(
    resid_in,
    queries,
    kv_cache,
    new_kv,
    lengths,
    out_weight,
    enc_weight,
    enc_bias,
    dec_weight,
    clamp_ids,
    clamp_values,
):
    f32, bf16 = jnp.float32, jnp.bfloat16
    tp_rank, grp_rank = lax.axis_index("tp"), lax.axis_index("grp")
    chip, core = tp_rank // 2, tp_rank % 2
    z, plane = grp_rank // 2, grp_rank % 2
    rows, width = resid_in.shape
    span = enc_weight.shape[1]
    quarter = 8192

    enc_other = swap_core(enc_weight)
    out_split = out_weight.reshape(out_weight.shape[0], 8, 2, width)
    out_mine = lax.dynamic_index_in_dim(out_split, core, 2, keepdims=False)
    out_give = lax.dynamic_index_in_dim(out_split, 1 - core, 2, keepdims=False)
    out_take = swap_core(out_give)

    heads_mine = attend(queries, kv_cache, new_kv, lengths, tp_rank // 4)
    heads_other = swap_core(heads_mine)
    part = jnp.einsum("sk,kdn->dsn", heads_mine, out_mine, preferred_element_type=f32)
    part = part + jnp.einsum("sk,kdn->dsn", heads_other, out_take, preferred_element_type=f32)
    groups = [[c + 2 * i for i in range(8)] for c in range(2)]
    arrived = lax.all_to_all(
        part.astype(bf16), "tp", 0, 0, axis_index_groups=groups, tiled=True
    )
    resid_mid = (resid_in.astype(f32) + jnp.sum(arrived.astype(f32), axis=0)).astype(bf16)

    both = jnp.concatenate([resid_mid, swap_core(resid_mid)], axis=1)
    first_id = clamp_ids[:, :1]
    id_parts = jnp.concatenate([first_id // 256, first_id % 256], axis=1).astype(bf16)
    both = jnp.concatenate([both, jnp.pad(id_parts, ((0, 0), (0, 126)))], axis=1)
    cross = [
        (t * 16 + z_ * 2 + t % 2, t * 16 + z_ * 2 + 1 - t % 2) for t in range(16) for z_ in range(8)
    ]
    crossed = lax.ppermute(both, ("tp", "grp"), cross)
    block = [None] * 8
    block[0] = jnp.where(core == plane, both, crossed)
    block[1], block[7] = from_z(block[0], 1), from_z(block[0], 7)
    block[2], block[6] = from_z(block[0], 2), from_z(block[0], 6)
    block[3], block[5] = from_z(block[2], 1), from_z(block[6], 7)
    block[4] = from_z(block[2], 2)
    stack = jnp.stack(block)

    offsets = [(1, 2), (1, 1), (1, 3), (1, 0), (0, 2), (0, 1), (0, 3), (0, 0)]
    order = [((chip // 4 + dx) % 2 * 4 + (chip + dy) % 4 - z) % 8 for dx, dy in offsets]
    picked = jnp.concatenate(
        [lax.dynamic_index_in_dim(stack, k, 0, keepdims=False)[:, : 2 * width] for k in order]
    )
    pre_part = mm(picked[:, :width], enc_weight) + mm(picked[:, width:], enc_other)
    pre_part = pre_part.astype(bf16).reshape(8, rows, span)
    total = pre_part[7].astype(f32)
    for i, (dx, dy) in enumerate(offsets[:7]):
        total = total + to_chip(pre_part[i], dx, dy).astype(f32)
    features = jnp.maximum(total + enc_bias, 0.0).astype(bf16)

    id_pair = stack[:, :, 2 * width : 2 * width + 2].astype(jnp.int32)
    ids_here = id_pair[..., 0] * 256 + id_pair[..., 1]
    ids_there = swap_core(ids_here)
    ids = jnp.where(core == 0, jnp.stack([ids_here, ids_there], 1), jnp.stack([ids_there, ids_here], 1))

    my_quarter = grp_rank // 4
    want = ids % quarter + my_quarter * quarter - grp_rank * span
    parity = z % 2
    take = lambda p, s: jnp.concatenate(
        [
            lax.dynamic_index_in_dim(
                lax.dynamic_index_in_dim(want, (2 * k + p - parity) % 8, 0, keepdims=False),
                s, 0, keepdims=False,
            )
            for k in range(4)
        ]
    )
    ordered = jnp.concatenate(
        [take(1 - parity, 1 - plane), take(1 - parity, plane), take(parity, 1 - plane), take(parity, plane)]
    )
    hits = (ordered[:, None] == jnp.arange(span, dtype=jnp.int32)[None, :]).astype(bf16)
    found = mm(hits, dec_weight).astype(bf16)
    near = lax.ppermute(
        found[: 8 * rows], "grp", grp_moves(lambda z_, s: (z_ ^ 1) * 2 + s)
    )
    found = found[8 * rows :] + near
    near = lax.ppermute(
        found[: 4 * rows], "grp", grp_moves(lambda z_, s: z_ * 2 + 1 - s)
    )
    found = (found[4 * rows :] + near).reshape(4, rows, width)
    dec_rows = [found[0]] + [from_z(found[k], -2 * k) for k in range(1, 4)]

    mine = lax.dynamic_index_in_dim(want, (chip - z) % 8, 0, keepdims=False)
    mine = lax.dynamic_index_in_dim(mine, core, 0, keepdims=False)
    hit = mine[:, None] == jnp.arange(span, dtype=jnp.int32)[None, :]
    now = jnp.sum(jnp.where(hit, features.astype(f32), 0.0), axis=1)
    swapped = lax.ppermute(
        now.reshape(1, rows), ("tp", "grp"), [(t * 16 + g, g * 16 + t) for t in range(16) for g in range(16)]
    )
    every = lax.all_to_all(
        jnp.broadcast_to(swapped[None], (16, 1, rows)), "tp", 0, 0, tiled=True
    ).reshape(4, 4, rows).sum(axis=1)
    edit = jnp.zeros((rows, width), f32)
    own_quarter = clamp_ids // quarter
    for k in range(4):
        q = (my_quarter - k) % 4
        value = jnp.sum(jnp.where(own_quarter == q, clamp_values, 0.0), axis=1)
        delta = (value - lax.dynamic_index_in_dim(every, q, 0, keepdims=False)).astype(bf16)
        edit = edit + delta.astype(f32)[:, None] * dec_rows[k].astype(f32)
    resid_out = (resid_mid.astype(f32) + edit).astype(bf16)
    return (resid_out, features)


def solution(mesh):
    placed = (
        P("grp", "tp"),
        P("grp", "tp"),
        P(None, "grp", "tp", None, None),
        P(None, "grp", None, None),
        P("grp"),
        P("tp", None),
        P("tp", "grp"),
        P("grp"),
        P("grp", "tp"),
        P("grp", None),
        P("grp", None),
    )
    return jax.shard_map(
        per_device,
        mesh=mesh,
        in_specs=placed,
        out_specs=(P("grp", "tp"), P("tp", "grp")),
        check_vma=False,
    )
```

```python
import jax
import jax.numpy as jnp
from jax import lax
from jax.experimental import pallas as pl
from jax.experimental.pallas import tpu as pltpu
from jax.experimental import pallas as pl
from jax.experimental.pallas import tpu as pltpu
from jax.sharding import PartitionSpec as P

HEAD_DIM = 128
QUARTER = 8192


def tp_moves(move):
    return [(chip * 2 + core, move(chip, core)) for chip in range(8) for core in range(2)]


def grp_moves(move):
    return [(z * 2 + plane, move(z, plane)) for z in range(8) for plane in range(2)]


def swap_core(value):
    return lax.ppermute(value, "tp", tp_moves(lambda chip, core: chip * 2 + 1 - core))


def from_z(value, ahead):
    return lax.ppermute(
        value, "grp", grp_moves(lambda z, plane: (z - ahead) % 8 * 2 + plane)
    )


def chip_at(chip, dx, dy):
    return (chip // 4 + dx) % 2 * 4 + (chip + dy) % 4


def to_chip(value, dx, dy):
    return lax.ppermute(
        value, "tp", tp_moves(lambda chip, core: chip_at(chip, dx, dy) * 2 + core)
    )


def attend(queries, kv_cache, new_kv, lengths, kv_index):
    row_count = queries.shape[0]
    own_heads = queries.shape[1] // HEAD_DIM
    slot_count = kv_cache.shape[3]
    score_scale = HEAD_DIM ** (-0.5)
    query_heads = queries.reshape(row_count, own_heads, HEAD_DIM)
    cache_keys = kv_cache[0, :, 0]
    cache_values = kv_cache[1, :, 0]
    new_key = lax.dynamic_index_in_dim(new_kv[0], kv_index, 1, keepdims=False)
    new_value = lax.dynamic_index_in_dim(new_kv[1], kv_index, 1, keepdims=False)
    scores = (
        jnp.einsum("shd,spd->shp", query_heads, cache_keys, preferred_element_type=jnp.float32)
        * score_scale
    )
    new_score = (
        jnp.einsum("shd,sd->sh", query_heads, new_key, preferred_element_type=jnp.float32)
        * score_scale
    )
    slot_index = jnp.arange(slot_count, dtype=jnp.int32)
    is_valid = (slot_index[None, :] < lengths[:, None])[:, None, :]
    top_score = jnp.maximum(jnp.max(jnp.where(is_valid, scores, -jnp.inf), axis=-1), new_score)
    prob_cache = jnp.where(is_valid, jnp.exp(scores - top_score[..., None]), 0.0)
    new_prob = jnp.exp(new_score - top_score)
    total_weight = jnp.sum(prob_cache, axis=-1) + new_prob
    new_rounded = lax.optimization_barrier(new_prob.astype(jnp.bfloat16)).astype(jnp.float32)
    weighted = jnp.einsum(
        "shp,spd->shd",
        prob_cache.astype(jnp.bfloat16),
        cache_values,
        preferred_element_type=jnp.float32,
    )
    weighted = weighted + new_rounded[..., None] * new_value.astype(jnp.float32)[:, None, :]
    return (
        (weighted / total_weight[..., None])
        .astype(jnp.bfloat16)
        .reshape(row_count, own_heads * HEAD_DIM)
    )


def mm(a, b):
    return jnp.dot(a, b, preferred_element_type=jnp.float32)


def project_kernel(core_ref, mine_ref, other_ref, w_mine_ref, w_other_ref, out_ref):
    out_ref[0] = (mm(mine_ref[...], w_mine_ref[...]) + mm(other_ref[...], w_other_ref[...])).astype(
        out_ref.dtype
    )


def project(core, heads_mine, heads_other, w_mine, w_other, width):
    rows, depth = heads_mine.shape
    columns = lambda i, core_ref: (0, 2 * i + core_ref[0])
    whole = lambda i, core_ref: (0, 0)
    return pl.pallas_call(
        project_kernel,
        grid_spec=pltpu.PrefetchScalarGridSpec(
            num_scalar_prefetch=1,
            grid=(8,),
            in_specs=[
                pl.BlockSpec((rows, depth), whole),
                pl.BlockSpec((rows, depth), whole),
                pl.BlockSpec((depth, width), columns),
                pl.BlockSpec((depth, width), columns),
            ],
            out_specs=pl.BlockSpec((1, rows, width), lambda i, core_ref: (i, 0, 0)),
        ),
        out_shape=jax.ShapeDtypeStruct((8, rows, width), jnp.bfloat16),
        cost_estimate=pl.CostEstimate(
            flops=2 * rows * 2 * depth * 8 * width,
            bytes_accessed=2 * 2 * depth * 8 * width,
            transcendentals=0,
        ),
        name="project",
    )(core.reshape(1), heads_mine, heads_other, w_mine, w_other)


def encode_kernel(slot_ref, *refs):
    block_refs, (want_ref, bias_ref, w_mine_ref, w_other_ref) = refs[:8], refs[8:12]
    out_refs, x_ref = refs[12:21], refs[21]
    step = pl.program_id(0)
    half = w_mine_ref.shape[0]
    tile = w_mine_ref.shape[1]
    rows = out_refs[0].shape[0]

    @pl.when(step == 0)
    def _():
        for k in range(8):
            x_ref[pl.ds(pl.multiple_of(slot_ref[k] * rows, rows), rows), :] = block_refs[k][...]

    part = mm(x_ref[:, :half], w_mine_ref[...]) + mm(x_ref[:, half:], w_other_ref[...])
    part = part.astype(jnp.bfloat16)
    for slot in range(8):
        out_refs[slot][...] = part[slot * rows : (slot + 1) * rows]
    column = lax.broadcasted_iota(jnp.int32, part.shape, 1) + step * tile
    is_hit = column == want_ref[...]
    now = jnp.sum(
        jnp.where(is_hit, part.astype(jnp.float32) + bias_ref[...], 0.0), axis=1, keepdims=True
    )
    total_ref = out_refs[8]

    @pl.when(step == 0)
    def _():
        total_ref[...] = now

    @pl.when(step != 0)
    def _():
        total_ref[...] += now


def encode(block, slot, want, bias, w_mine, w_other):
    rows, depth = block[0].shape
    count = 8 * rows
    span = w_mine.shape[1]
    tile = 256
    return pl.pallas_call(
        encode_kernel,
        grid_spec=pltpu.PrefetchScalarGridSpec(
            num_scalar_prefetch=1,
            grid=(span // tile,),
            in_specs=[pl.BlockSpec((rows, depth), lambda i, slot: (0, 0))] * 8
            + [
                pl.BlockSpec((count, 1), lambda i, slot: (0, 0)),
                pl.BlockSpec((1, tile), lambda i, slot: (0, i)),
                pl.BlockSpec((depth // 2, tile), lambda i, slot: (0, i)),
                pl.BlockSpec((depth // 2, tile), lambda i, slot: (0, i)),
            ],
            out_specs=[pl.BlockSpec((rows, tile), lambda i, slot: (0, i))] * 8
            + [pl.BlockSpec((count, 1), lambda i, slot: (0, 0))],
            scratch_shapes=[pltpu.VMEM((count, depth), jnp.bfloat16)],
        ),
        out_shape=[jax.ShapeDtypeStruct((rows, span), jnp.bfloat16)] * 8
        + [jax.ShapeDtypeStruct((count, 1), jnp.float32)],
        cost_estimate=pl.CostEstimate(
            flops=2 * count * depth * span,
            bytes_accessed=2 * (depth * span + count * (depth + span)),
            transcendentals=0,
        ),
        name="encode",
    )(slot, *block, want, bias, w_mine, w_other)


def per_device(
    resid_in,
    queries,
    kv_cache,
    new_kv,
    lengths,
    out_weight,
    enc_weight,
    enc_bias,
    dec_weight,
    clamp_ids,
    clamp_values,
):
    f32, bf16 = jnp.float32, jnp.bfloat16
    tp_rank, grp_rank = lax.axis_index("tp"), lax.axis_index("grp")
    chip, core = tp_rank // 2, tp_rank % 2
    z, plane = grp_rank // 2, grp_rank % 2
    rows, width = resid_in.shape
    span = enc_weight.shape[1]
    my_quarter, parity = z // 2, z % 2

    ids = lax.all_to_all(
        jnp.broadcast_to(clamp_ids[:, 0].reshape(1, 1, rows), (16, 1, rows)), "grp", 0, 0, tiled=True
    ).reshape(16, rows)
    out_other = swap_core(out_weight)
    enc_other = swap_core(enc_weight)

    heads_mine = attend(queries, kv_cache, new_kv, lengths, tp_rank // 4)
    heads_other = swap_core(heads_mine)
    part = project(core, heads_mine, heads_other, out_weight, out_other, width)
    groups = [[c + 2 * i for i in range(8)] for c in range(2)]
    arrived = lax.all_to_all(part, "tp", 0, 0, axis_index_groups=groups, tiled=True)
    resid_mid = (resid_in.astype(f32) + jnp.sum(arrived.astype(f32), axis=0)).astype(bf16)

    want = ids % QUARTER + my_quarter * QUARTER - grp_rank * span
    ordered = want.reshape(4, 2, 2, rows).transpose(1, 2, 0, 3)
    ordered = jnp.where(parity == 1, ordered, ordered[::-1])
    ordered = jnp.where(plane == 1, ordered, ordered[:, ::-1]).reshape(16 * rows)
    hits = (ordered[:, None] == jnp.arange(span, dtype=jnp.int32)[None, :]).astype(bf16)
    found = mm(hits, dec_weight).astype(bf16)

    mid_other = swap_core(resid_mid)
    both = jnp.concatenate([resid_mid, mid_other], axis=1)
    cross = [
        (t * 16 + z_ * 2 + t % 2, t * 16 + z_ * 2 + 1 - t % 2) for t in range(16) for z_ in range(8)
    ]
    crossed = lax.ppermute(both, ("tp", "grp"), cross)
    near = lax.ppermute(found[: 8 * rows], "grp", grp_moves(lambda z_, s: (z_ ^ 1) * 2 + s))
    block = [None] * 8
    block[0] = jnp.where(core == plane, both, crossed)
    for k, source, step in (
        (1, 0, 1), (7, 0, 7), (2, 0, 2), (6, 0, 6),
        (3, 2, 1), (5, 6, 7), (4, 2, 2),
    ):
        block[k] = from_z(block[source], step)
    found = found[8 * rows :] + near
    near = lax.ppermute(found[: 4 * rows], "grp", grp_moves(lambda z_, s: z_ * 2 + 1 - s))
    found = (found[4 * rows :] + near).reshape(4, rows, width)
    dec_rows = [lax.dynamic_index_in_dim(found, my_quarter, 0, keepdims=False)]
    for k in (1, 2, 3):
        give = lax.dynamic_index_in_dim(found, (my_quarter + k) % 4, 0, keepdims=False)
        dec_rows.append(from_z(give, -2 * k))

    target = [chip_at(chip, s // 4, s % 4) for s in range(8)]
    ahead = (jnp.arange(8, dtype=jnp.int32) + z) % 8
    slot = (ahead // 4 + chip // 4) % 2 * 4 + (ahead - chip) % 4
    mine = lax.dynamic_index_in_dim(want.reshape(8, 2, rows), core, 1, keepdims=False)
    slots = jnp.concatenate([lax.dynamic_index_in_dim(mine, t, 0, keepdims=False) for t in target])
    bias = jnp.where(chip == 0, enc_bias, 0.0).reshape(1, span)
    outs = encode(block, slot, slots.reshape(8 * rows, 1), bias, enc_weight, enc_other)

    now = outs[8].reshape(8, rows)
    by_z = jnp.stack(
        [
            lax.dynamic_index_in_dim(now, chip_at(t, chip // 4, -chip % 4), 0, keepdims=False)
            for t in range(8)
        ]
    )
    sent = jnp.where(
        (jnp.arange(2) == core)[None, :, None], by_z[:, None, :], 0.0
    ).reshape(16, 1, rows)
    held = lax.all_to_all(sent, "grp", 0, 0, tiled=True)
    held = held.reshape(4, 4, rows).sum(axis=1)

    total = outs[0].astype(f32)
    moved = []
    for s in (6, 5, 7, 4, 2, 1, 3):
        moved.append(to_chip(outs[s], s // 4, s % 4))
    every = lax.all_to_all(
        jnp.broadcast_to(held[None], (16, 4, rows)), "tp", 0, 0, tiled=True
    )
    for value in moved:
        total = total + value.astype(f32)
    features = jnp.maximum(total + enc_bias, 0.0).astype(bf16)

    every = every.reshape(16, 4, rows).sum(axis=0)
    every = jnp.maximum(every, 0.0).astype(bf16).astype(f32)
    edit = jnp.zeros((rows, width), f32)
    own_quarter = clamp_ids // QUARTER
    for k in range(4):
        q = (my_quarter - k) % 4
        value = jnp.sum(jnp.where(own_quarter == q, clamp_values, 0.0), axis=1)
        delta = (value - lax.dynamic_index_in_dim(every, q, 0, keepdims=False)).astype(bf16)
        edit = edit + delta.astype(f32)[:, None] * dec_rows[k].astype(f32)
    resid_out = (resid_mid.astype(f32) + edit).astype(bf16)
    return (resid_out, features)


def solution(mesh):
    placed = (
        P("grp", "tp"),
        P("grp", "tp"),
        P(None, "grp", "tp", None, None),
        P(None, "grp", None, None),
        P("grp"),
        P("tp", None),
        P("tp", "grp"),
        P("grp"),
        P("grp", "tp"),
        P("grp", None),
        P("grp", None),
    )
    return jax.shard_map(
        per_device,
        mesh=mesh,
        in_specs=placed,
        out_specs=(P("grp", "tp"), P("tp", "grp")),
        check_vma=False,
    )
```

```python
import jax
import jax.numpy as jnp
from jax import lax
from jax.experimental import pallas as pl
from jax.experimental.pallas import tpu as pltpu
from jax.experimental import pallas as pl
from jax.experimental.pallas import tpu as pltpu
from jax.sharding import PartitionSpec as P

HEAD_DIM = 128
QUARTER = 8192


def tp_moves(move):
    return [(chip * 2 + core, move(chip, core)) for chip in range(8) for core in range(2)]


def grp_moves(move):
    return [(z * 2 + plane, move(z, plane)) for z in range(8) for plane in range(2)]


def swap_core(value):
    return lax.ppermute(value, "tp", tp_moves(lambda chip, core: chip * 2 + 1 - core))


def from_z(value, ahead):
    return lax.ppermute(
        value, "grp", grp_moves(lambda z, plane: (z - ahead) % 8 * 2 + plane)
    )


def flip_z(value, k):
    return lax.ppermute(value, "grp", grp_moves(lambda z, plane: (z ^ k) * 2 + plane))


def flip_plane(value):
    return lax.ppermute(value, "grp", grp_moves(lambda z, plane: z * 2 + 1 - plane))


def chip_at(chip, dx, dy):
    return (chip // 4 + dx) % 2 * 4 + (chip + dy) % 4


def to_chip(value, dx, dy):
    return lax.ppermute(
        value, "tp", tp_moves(lambda chip, core: chip_at(chip, dx, dy) * 2 + core)
    )


def attend(queries, kv_cache, new_kv, lengths, kv_index):
    row_count = queries.shape[0]
    own_heads = queries.shape[1] // HEAD_DIM
    slot_count = kv_cache.shape[3]
    score_scale = HEAD_DIM ** (-0.5)
    query_heads = queries.reshape(row_count, own_heads, HEAD_DIM)
    cache_keys = kv_cache[0, :, 0]
    cache_values = kv_cache[1, :, 0]
    new_key = lax.dynamic_index_in_dim(new_kv[0], kv_index, 1, keepdims=False)
    new_value = lax.dynamic_index_in_dim(new_kv[1], kv_index, 1, keepdims=False)
    scores = (
        jnp.einsum("shd,spd->shp", query_heads, cache_keys, preferred_element_type=jnp.float32)
        * score_scale
    )
    new_score = (
        jnp.einsum("shd,sd->sh", query_heads, new_key, preferred_element_type=jnp.float32)
        * score_scale
    )
    slot_index = jnp.arange(slot_count, dtype=jnp.int32)
    is_valid = (slot_index[None, :] < lengths[:, None])[:, None, :]
    top_score = jnp.maximum(jnp.max(jnp.where(is_valid, scores, -jnp.inf), axis=-1), new_score)
    prob_cache = jnp.where(is_valid, jnp.exp(scores - top_score[..., None]), 0.0)
    new_prob = jnp.exp(new_score - top_score)
    total_weight = jnp.sum(prob_cache, axis=-1) + new_prob
    new_rounded = lax.optimization_barrier(new_prob.astype(jnp.bfloat16)).astype(jnp.float32)
    weighted = jnp.einsum(
        "shp,spd->shd",
        prob_cache.astype(jnp.bfloat16),
        cache_values,
        preferred_element_type=jnp.float32,
    )
    weighted = weighted + new_rounded[..., None] * new_value.astype(jnp.float32)[:, None, :]
    return (
        (weighted / total_weight[..., None])
        .astype(jnp.bfloat16)
        .reshape(row_count, own_heads * HEAD_DIM)
    )


def mm(a, b):
    return jnp.dot(a, b, preferred_element_type=jnp.float32)


def project_kernel(core_ref, mine_ref, other_ref, *refs):
    weight_refs, out_ref = refs[:4], refs[4]
    for i in range(2):
        out_ref[i] = (
            mm(mine_ref[...], weight_refs[i][...]) + mm(other_ref[...], weight_refs[2 + i][...])
        ).astype(out_ref.dtype)


def project(core, heads_mine, heads_other, w_mine, w_other, width):
    rows, depth = heads_mine.shape
    columns = [pl.BlockSpec((depth, width), lambda i, core_ref, e=e: (0, 4 * i + 2 * e + core_ref[0])) for e in range(2)]
    whole = pl.BlockSpec((rows, depth), lambda i, core_ref: (0, 0))
    return pl.pallas_call(
        project_kernel,
        grid_spec=pltpu.PrefetchScalarGridSpec(
            num_scalar_prefetch=1,
            grid=(4,),
            in_specs=[whole, whole] + columns + columns,
            out_specs=pl.BlockSpec((2, rows, width), lambda i, core_ref: (i, 0, 0)),
        ),
        out_shape=jax.ShapeDtypeStruct((8, rows, width), jnp.bfloat16),
        cost_estimate=pl.CostEstimate(
            flops=2 * rows * 2 * depth * 8 * width,
            bytes_accessed=2 * 2 * depth * 8 * width,
            transcendentals=0,
        ),
        name="project",
    )(core.reshape(1), heads_mine, heads_other, w_mine, w_mine, w_other, w_other)


def select_kernel(dec_want_ref, enc_want_ref, dec_ref, enc_ref, bias_ref, dec_out_ref, enc_out_ref):
    width = dec_ref.shape[1]
    column = lax.broadcasted_iota(jnp.int32, (dec_want_ref.shape[0], dec_ref.shape[0]), 1)
    hits = (column == dec_want_ref[...]).astype(jnp.float32).astype(jnp.bfloat16)
    dec_out_ref[...] = mm(hits, dec_ref[...]).astype(jnp.bfloat16)
    hits = (column == enc_want_ref[...]).astype(jnp.float32).astype(jnp.bfloat16)
    across = lambda a, b: lax.dot_general(
        a, b, (((1,), (1,)), ((), ())), preferred_element_type=jnp.float32
    )
    enc_out_ref[:, :width] = across(hits, enc_ref[...]).astype(jnp.bfloat16)
    enc_out_ref[:, width:] = across(hits, bias_ref[...]).astype(jnp.bfloat16)


def select(dec_want, enc_want, dec_weight, enc_weight, bias_parts):
    count, tile = dec_want.shape[0], 256
    span, width = dec_weight.shape
    lanes = bias_parts.shape[0]
    fixed = lambda shape: pl.BlockSpec(shape, lambda i: (0, 0), pipeline_mode=pl.Buffered(1))
    return pl.pallas_call(
        select_kernel,
        grid=(count // tile,),
        in_specs=[
            pl.BlockSpec((tile, 1), lambda i: (i, 0)),
            pl.BlockSpec((tile, 1), lambda i: (i, 0)),
            fixed((span, width)),
            fixed((width, span)),
            fixed((lanes, span)),
        ],
        out_specs=[
            pl.BlockSpec((tile, width), lambda i: (i, 0)),
            pl.BlockSpec((tile, width + lanes), lambda i: (i, 0)),
        ],
        out_shape=[
            jax.ShapeDtypeStruct((count, width), jnp.bfloat16),
            jax.ShapeDtypeStruct((count, width + lanes), jnp.bfloat16),
        ],
        cost_estimate=pl.CostEstimate(
            flops=2 * count * span * (2 * width + lanes),
            bytes_accessed=2 * span * (2 * width + lanes) + 2 * count * (2 * width + lanes),
            transcendentals=0,
        ),
        name="select",
    )(dec_want, enc_want, dec_weight, enc_weight, bias_parts)


def encode_kernel(slot_ref, *refs):
    block_refs, (w_mine_ref, w_other_ref) = refs[:8], refs[8:10]
    out_refs, x_ref = refs[10:18], refs[18]
    half = w_mine_ref.shape[0]
    rows = out_refs[0].shape[0]

    @pl.when(pl.program_id(0) == 0)
    def _():
        for k in range(8):
            x_ref[pl.ds(pl.multiple_of(slot_ref[k] * rows, rows), rows), :] = block_refs[k][...]

    part = mm(x_ref[:, :half], w_mine_ref[...]) + mm(x_ref[:, half:], w_other_ref[...])
    part = part.astype(jnp.bfloat16)
    for slot in range(8):
        out_refs[slot][...] = part[slot * rows : (slot + 1) * rows]


def encode(block, slot, w_mine, w_other):
    rows, depth = block[0].shape
    count = 8 * rows
    span = w_mine.shape[1]
    tile = 512
    return pl.pallas_call(
        encode_kernel,
        grid_spec=pltpu.PrefetchScalarGridSpec(
            num_scalar_prefetch=1,
            grid=(span // tile,),
            in_specs=[pl.BlockSpec((rows, depth), lambda i, slot: (0, 0))] * 8
            + [pl.BlockSpec((depth // 2, tile), lambda i, slot: (0, i))] * 2,
            out_specs=[pl.BlockSpec((rows, tile), lambda i, slot: (0, i))] * 8,
            scratch_shapes=[pltpu.VMEM((count, depth), jnp.bfloat16)],
        ),
        out_shape=[jax.ShapeDtypeStruct((rows, span), jnp.bfloat16)] * 8,
        cost_estimate=pl.CostEstimate(
            flops=2 * count * depth * span,
            bytes_accessed=2 * (depth * span + count * (depth + span)),
            transcendentals=0,
        ),
        name="encode",
    )(slot, *block, w_mine, w_other)


def per_device(
    resid_in,
    queries,
    kv_cache,
    new_kv,
    lengths,
    out_weight,
    enc_weight,
    enc_bias,
    dec_weight,
    clamp_ids,
    clamp_values,
):
    f32, bf16 = jnp.float32, jnp.bfloat16
    tp_rank, grp_rank = lax.axis_index("tp"), lax.axis_index("grp")
    chip, core = tp_rank // 2, tp_rank % 2
    z, plane = grp_rank // 2, grp_rank % 2
    rows, width = resid_in.shape
    span = enc_weight.shape[1]
    my_quarter = z // 2

    ids = clamp_ids[:, :1].reshape(1, rows)
    ids = jnp.concatenate([ids, flip_plane(ids)])
    for k in (1, 2, 4):
        ids = jnp.concatenate([ids, flip_z(ids, k)])

    out_other = swap_core(out_weight)
    enc_other = swap_core(enc_weight)

    heads_mine = attend(queries, kv_cache, new_kv, lengths, tp_rank // 4)
    heads_other = swap_core(heads_mine)
    part = project(core, heads_mine, heads_other, out_weight, out_other, width)
    groups = [[c + 2 * i for i in range(8)] for c in range(2)]
    arrived = lax.all_to_all(part, "tp", 0, 0, axis_index_groups=groups, tiled=True)
    resid_mid = (resid_in.astype(f32) + jnp.sum(arrived.astype(f32), axis=0)).astype(bf16)

    want = (ids % QUARTER + my_quarter * QUARTER - grp_rank * span).reshape(4, 2, 2, rows)
    want = want[:, ::-1, ::-1]
    dec_want = want.transpose(1, 2, 0, 3).reshape(16 * rows, 1)
    enc_want = want.transpose(2, 1, 0, 3).reshape(16 * rows, 1)
    high = enc_bias.astype(bf16)
    middle = (enc_bias - high.astype(f32)).astype(bf16)
    low = (enc_bias - high.astype(f32) - middle.astype(f32)).astype(bf16)
    bias_parts = jnp.pad(jnp.stack([high, middle, low]), ((0, 125), (0, 0)))
    found_dec, found_enc = select(dec_want, enc_want, dec_weight, enc_weight, bias_parts)
    near_dec = flip_z(found_dec[: 8 * rows], 1)
    near_enc = flip_plane(found_enc[: 8 * rows])

    mid_other = swap_core(resid_mid)
    both = jnp.concatenate([resid_mid, mid_other], axis=1)
    cross = [
        (t * 16 + z_ * 2 + t % 2, t * 16 + z_ * 2 + 1 - t % 2) for t in range(16) for z_ in range(8)
    ]
    crossed = lax.ppermute(both, ("tp", "grp"), cross)
    block = [None] * 8
    block[0] = jnp.where(core == plane, both, crossed)
    for k, source, step in (
        (1, 0, 1), (7, 0, 7), (2, 0, 2), (6, 0, 6),
        (3, 2, 1), (5, 6, 7), (4, 2, 2),
    ):
        block[k] = from_z(block[source], step)
    found_dec = found_dec[8 * rows :] + near_dec
    found_enc = found_enc[8 * rows :] + near_enc
    near_dec = flip_plane(found_dec[: 4 * rows])
    near_enc = flip_z(found_enc[: 4 * rows], 1)
    found = jnp.concatenate([found_dec[4 * rows :] + near_dec, found_enc[4 * rows :] + near_enc], axis=1)
    held = [found[:rows]]
    for k in (1, 2, 3):
        held.append(flip_z(found[k * rows : (k + 1) * rows], 2 * k))

    ahead = (jnp.arange(8, dtype=jnp.int32) + z) % 8
    slot = (ahead // 4 + chip // 4) % 2 * 4 + (ahead - chip) % 4
    outs = encode(block, slot, enc_weight, enc_other)

    total = outs[0].astype(f32)
    moved = []
    for s in (6, 5, 7, 4, 2, 1, 3):
        moved.append(to_chip(outs[s], s // 4, s % 4))

    mid_again = lax.optimization_barrier(resid_mid).astype(f32)
    dots = jnp.stack(
        [
            jnp.sum(mid_again * h[:, width : 2 * width].astype(f32), axis=1)
            for h in held
        ]
    )
    every = lax.all_to_all(
        jnp.broadcast_to(dots[None], (16, 4, rows)), "tp", 0, 0, tiled=True
    )
    for value in moved:
        total = total + value.astype(f32)
    features = jnp.maximum(total + enc_bias, 0.0).astype(bf16)

    every = every.reshape(16, 4, rows).sum(axis=0)
    edit = jnp.zeros((rows, width), f32)
    own_quarter = clamp_ids // QUARTER
    for k in range(4):
        value = jnp.sum(jnp.where(own_quarter == my_quarter ^ k, clamp_values, 0.0), axis=1)
        bias = jnp.sum(held[k][:, 2 * width :].astype(f32), axis=1)
        now = jnp.maximum(every[k] + bias, 0.0).astype(bf16).astype(f32)
        delta = (value - now).astype(bf16).astype(f32)
        edit = edit + delta[:, None] * held[k][:, :width].astype(f32)
    resid_out = (resid_mid.astype(f32) + edit).astype(bf16)
    return (resid_out, features)


def solution(mesh):
    placed = (
        P("grp", "tp"),
        P("grp", "tp"),
        P(None, "grp", "tp", None, None),
        P(None, "grp", None, None),
        P("grp"),
        P("tp", None),
        P("tp", "grp"),
        P("grp"),
        P("grp", "tp"),
        P("grp", None),
        P("grp", None),
    )
    return jax.shard_map(
        per_device,
        mesh=mesh,
        in_specs=placed,
        out_specs=(P("grp", "tp"), P("tp", "grp")),
        check_vma=False,
    )
```

```python
import jax
import jax.numpy as jnp
from jax import lax
from jax.experimental import pallas as pl
from jax.experimental.pallas import tpu as pltpu
from jax.experimental import pallas as pl
from jax.experimental.pallas import tpu as pltpu
from jax.sharding import PartitionSpec as P

HEAD_DIM = 128
QUARTER = 8192


def tp_moves(move):
    return [(chip * 2 + core, move(chip, core)) for chip in range(8) for core in range(2)]


def grp_moves(move):
    return [(z * 2 + plane, move(z, plane)) for z in range(8) for plane in range(2)]


def swap_core(value):
    return lax.ppermute(value, "tp", tp_moves(lambda chip, core: chip * 2 + 1 - core))


def from_z(value, ahead):
    return lax.ppermute(
        value, "grp", grp_moves(lambda z, plane: (z - ahead) % 8 * 2 + plane)
    )


def flip_z(value, k):
    return lax.ppermute(value, "grp", grp_moves(lambda z, plane: (z ^ k) * 2 + plane))


def flip_plane(value):
    return lax.ppermute(value, "grp", grp_moves(lambda z, plane: z * 2 + 1 - plane))


def chip_at(chip, dx, dy):
    return (chip // 4 + dx) % 2 * 4 + (chip + dy) % 4


def to_chip(value, dx, dy):
    return lax.ppermute(
        value, "tp", tp_moves(lambda chip, core: chip_at(chip, dx, dy) * 2 + core)
    )


def attend(queries, kv_cache, new_kv, lengths, kv_index):
    row_count = queries.shape[0]
    own_heads = queries.shape[1] // HEAD_DIM
    slot_count = kv_cache.shape[3]
    score_scale = HEAD_DIM ** (-0.5)
    query_heads = queries.reshape(row_count, own_heads, HEAD_DIM)
    cache_keys = kv_cache[0, :, 0]
    cache_values = kv_cache[1, :, 0]
    new_key = lax.dynamic_index_in_dim(new_kv[0], kv_index, 1, keepdims=False)
    new_value = lax.dynamic_index_in_dim(new_kv[1], kv_index, 1, keepdims=False)
    scores = (
        jnp.einsum("shd,spd->shp", query_heads, cache_keys, preferred_element_type=jnp.float32)
        * score_scale
    )
    new_score = (
        jnp.einsum("shd,sd->sh", query_heads, new_key, preferred_element_type=jnp.float32)
        * score_scale
    )
    slot_index = jnp.arange(slot_count, dtype=jnp.int32)
    is_valid = (slot_index[None, :] < lengths[:, None])[:, None, :]
    top_score = jnp.maximum(jnp.max(jnp.where(is_valid, scores, -jnp.inf), axis=-1), new_score)
    prob_cache = jnp.where(is_valid, jnp.exp(scores - top_score[..., None]), 0.0)
    new_prob = jnp.exp(new_score - top_score)
    total_weight = jnp.sum(prob_cache, axis=-1) + new_prob
    new_rounded = lax.optimization_barrier(new_prob.astype(jnp.bfloat16)).astype(jnp.float32)
    weighted = jnp.einsum(
        "shp,spd->shd",
        prob_cache.astype(jnp.bfloat16),
        cache_values,
        preferred_element_type=jnp.float32,
    )
    weighted = weighted + new_rounded[..., None] * new_value.astype(jnp.float32)[:, None, :]
    return (
        (weighted / total_weight[..., None])
        .astype(jnp.bfloat16)
        .reshape(row_count, own_heads * HEAD_DIM)
    )


def mm(a, b):
    return jnp.dot(a, b, preferred_element_type=jnp.float32)


def project_kernel(core_ref, mine_ref, other_ref, *refs):
    weight_refs, out_ref = refs[:4], refs[4]
    for i in range(2):
        out_ref[i] = (
            mm(mine_ref[...], weight_refs[i][...]) + mm(other_ref[...], weight_refs[2 + i][...])
        ).astype(out_ref.dtype)


def project(core, heads_mine, heads_other, w_mine, w_other, width):
    rows, depth = heads_mine.shape
    columns = [pl.BlockSpec((depth, width), lambda i, core_ref, e=e: (0, 4 * i + 2 * e + core_ref[0])) for e in range(2)]
    whole = pl.BlockSpec((rows, depth), lambda i, core_ref: (0, 0))
    return pl.pallas_call(
        project_kernel,
        grid_spec=pltpu.PrefetchScalarGridSpec(
            num_scalar_prefetch=1,
            grid=(4,),
            in_specs=[whole, whole] + columns + columns,
            out_specs=pl.BlockSpec((2, rows, width), lambda i, core_ref: (i, 0, 0)),
        ),
        out_shape=jax.ShapeDtypeStruct((8, rows, width), jnp.bfloat16),
        cost_estimate=pl.CostEstimate(
            flops=2 * rows * 2 * depth * 8 * width,
            bytes_accessed=2 * 2 * depth * 8 * width,
            transcendentals=0,
        ),
        name="project",
    )(core.reshape(1), heads_mine, heads_other, w_mine, w_mine, w_other, w_other)


def select_kernel(grp_ref, *refs):
    want_refs, (dec_ref, enc_ref, bias_ref) = refs[:4], refs[4:7]
    dec_give_ref, dec_keep_ref, enc_give_ref, enc_keep_ref = refs[7:]
    want = jnp.concatenate([ref[0] for ref in want_refs])
    column = lax.broadcasted_iota(jnp.int32, (want.shape[0], dec_ref.shape[0]), 1)
    hits = (column == want).astype(jnp.float32).astype(jnp.bfloat16)
    across = lambda a, b: lax.dot_general(
        a, b, (((1,), (1,)), ((), ())), preferred_element_type=jnp.float32
    )
    dec = mm(hits, dec_ref[...]).astype(jnp.bfloat16)
    enc = across(hits, enc_ref[...]).astype(jnp.bfloat16)
    bias = across(hits, bias_ref[...]).astype(jnp.bfloat16)
    step = pl.program_id(0)

    def put(wanted, ref, values):
        @pl.when(wanted)
        def _():
            at = 0
            for value in values:
                ref[:, at : at + value.shape[1]] = value
                at += value.shape[1]

    put(step < 2, dec_give_ref, [dec])
    put(step >= 2, dec_keep_ref, [dec])
    put(step % 2 == 0, enc_give_ref, [enc, bias])
    put(step % 2 == 1, enc_keep_ref, [enc, bias])


def select(grp_rank, want, dec_weight, enc_weight, bias_parts):
    rows = want.shape[1]
    tile = 4 * rows
    span, width = dec_weight.shape
    lanes = bias_parts.shape[0]
    fixed = lambda shape: pl.BlockSpec(shape, lambda i, g: (0, 0), pipeline_mode=pl.Buffered(1))
    wanted = lambda k: pl.BlockSpec(
        (1, rows, 1), lambda i, g: (g[0] ^ (4 * k + 2 * (1 - i // 2) + 1 - i % 2), 0, 0)
    )
    half = lambda cols: jax.ShapeDtypeStruct((2 * tile, cols), jnp.bfloat16)
    return pl.pallas_call(
        select_kernel,
        grid_spec=pltpu.PrefetchScalarGridSpec(
            num_scalar_prefetch=1,
            grid=(4,),
            in_specs=[wanted(k) for k in range(4)]
            + [fixed((span, width)), fixed((width, span)), fixed((lanes, span))],
            out_specs=[
                pl.BlockSpec((tile, width), lambda i, g: (jnp.minimum(i, 1), 0)),
                pl.BlockSpec((tile, width), lambda i, g: (jnp.maximum(i - 2, 0), 0)),
                pl.BlockSpec((tile, width + lanes), lambda i, g: (i // 2, 0)),
                pl.BlockSpec((tile, width + lanes), lambda i, g: (i // 3, 0)),
            ],
        ),
        out_shape=[half(width), half(width), half(width + lanes), half(width + lanes)],
        cost_estimate=pl.CostEstimate(
            flops=8 * tile * span * (2 * width + lanes),
            bytes_accessed=2 * (span + 4 * tile) * (2 * width + lanes),
            transcendentals=0,
        ),
        name="select",
    )(grp_rank.reshape(1), want, want, want, want, dec_weight, enc_weight, bias_parts)


def encode_kernel(slot_ref, *refs):
    block_refs, (w_mine_ref, w_other_ref) = refs[:8], refs[8:10]
    out_refs, x_ref, sems = refs[10:18], refs[18], refs[19]
    half = w_mine_ref.shape[0]
    rows = out_refs[0].shape[0]

    @pl.when(pl.program_id(0) == 0)
    def _():
        copies = [
            pltpu.make_async_copy(
                block_refs[k],
                x_ref.at[pl.ds(pl.multiple_of(slot_ref[k] * rows, rows), rows), :],
                sems.at[k],
            )
            for k in range(8)
        ]
        for copy in copies:
            copy.start()
        for copy in copies:
            copy.wait()

    part = mm(x_ref[:, :half], w_mine_ref[...]) + mm(x_ref[:, half:], w_other_ref[...])
    part = part.astype(jnp.bfloat16)
    for slot in range(8):
        out_refs[slot][...] = part[slot * rows : (slot + 1) * rows]


def encode(block, slot, w_mine, w_other):
    rows, depth = block[0].shape
    count = 8 * rows
    span = w_mine.shape[1]
    tile = 512
    return pl.pallas_call(
        encode_kernel,
        grid_spec=pltpu.PrefetchScalarGridSpec(
            num_scalar_prefetch=1,
            grid=(span // tile,),
            in_specs=[pl.BlockSpec(memory_space=pl.ANY)] * 8
            + [pl.BlockSpec((depth // 2, tile), lambda i, slot: (0, i))] * 2,
            out_specs=[pl.BlockSpec((rows, tile), lambda i, slot: (0, i))] * 8,
            scratch_shapes=[
                pltpu.VMEM((count, depth), jnp.bfloat16),
                pltpu.SemaphoreType.DMA((8,)),
            ],
        ),
        out_shape=[jax.ShapeDtypeStruct((rows, span), jnp.bfloat16)] * 8,
        cost_estimate=pl.CostEstimate(
            flops=2 * count * depth * span,
            bytes_accessed=2 * (depth * span + count * (depth + span)),
            transcendentals=0,
        ),
        name="encode",
    )(slot, *block, w_mine, w_other)


def per_device(
    resid_in,
    queries,
    kv_cache,
    new_kv,
    lengths,
    out_weight,
    enc_weight,
    enc_bias,
    dec_weight,
    clamp_ids,
    clamp_values,
):
    f32, bf16 = jnp.float32, jnp.bfloat16
    tp_rank, grp_rank = lax.axis_index("tp"), lax.axis_index("grp")
    chip, core = tp_rank // 2, tp_rank % 2
    z, plane = grp_rank // 2, grp_rank % 2
    rows, width = resid_in.shape
    span = enc_weight.shape[1]
    my_quarter = z // 2

    ids = lax.all_to_all(
        jnp.broadcast_to(clamp_ids[:, 0].reshape(1, 1, rows), (16, 1, rows)), "grp", 0, 0, tiled=True
    ).reshape(16, rows, 1)

    out_other = swap_core(out_weight)
    enc_other = swap_core(enc_weight)

    heads_mine = attend(queries, kv_cache, new_kv, lengths, tp_rank // 4)
    heads_other = swap_core(heads_mine)
    part = project(core, heads_mine, heads_other, out_weight, out_other, width)
    groups = [[c + 2 * i for i in range(8)] for c in range(2)]
    arrived = lax.all_to_all(part, "tp", 0, 0, axis_index_groups=groups, tiled=True)
    resid_mid = (resid_in.astype(f32) + jnp.sum(arrived.astype(f32), axis=0)).astype(bf16)

    want = ids % QUARTER + (my_quarter * QUARTER - grp_rank * span)
    high = enc_bias.astype(bf16)
    middle = (enc_bias - high.astype(f32)).astype(bf16)
    low = (enc_bias - high.astype(f32) - middle.astype(f32)).astype(bf16)
    bias_parts = jnp.pad(jnp.stack([high, middle, low]), ((0, 125), (0, 0)))
    dec_give, dec_keep, enc_give, enc_keep = select(
        grp_rank, want, dec_weight, enc_weight, bias_parts
    )
    dec_near = flip_z(dec_give, 1)
    enc_near = flip_plane(enc_give)

    mid_other = swap_core(resid_mid)
    both = jnp.concatenate([resid_mid, mid_other], axis=1)
    cross = [
        (t * 16 + z_ * 2 + t % 2, t * 16 + z_ * 2 + 1 - t % 2) for t in range(16) for z_ in range(8)
    ]
    crossed = lax.ppermute(both, ("tp", "grp"), cross)
    block = [None] * 8
    block[0] = jnp.where(core == plane, both, crossed)
    for k, source, step in (
        (1, 0, 1), (7, 0, 7), (2, 0, 2), (6, 0, 6),
        (3, 2, 1), (5, 6, 7), (4, 2, 2),
    ):
        block[k] = from_z(block[source], step)
    first, last = slice(0, 4 * rows), slice(4 * rows, 8 * rows)
    dec_near_2 = flip_plane(dec_keep[first] + dec_near[first])
    enc_near_2 = flip_z(enc_keep[first] + enc_near[first], 1)
    dec_sum = dec_keep[last] + dec_near[last] + dec_near_2
    enc_sum = enc_keep[last] + enc_near[last] + enc_near_2
    held = []
    for k in range(4):
        piece = slice(k * rows, (k + 1) * rows)
        piece = jnp.concatenate([dec_sum[piece], enc_sum[piece]], axis=1)
        if k:
            piece = flip_z(piece, 2 * k)
        held.append(piece)

    ahead = (jnp.arange(8, dtype=jnp.int32) + z) % 8
    slot = (ahead // 4 + chip // 4) % 2 * 4 + (ahead - chip) % 4
    outs = encode(block, slot, enc_weight, enc_other)

    mid_again = lax.optimization_barrier(resid_mid).astype(f32)
    dots = jnp.stack(
        [
            jnp.sum(mid_again * h[:, width : 2 * width].astype(f32), axis=1)
            for h in held
        ]
    )
    every = lax.all_to_all(
        jnp.broadcast_to(dots[None], (16, 4, rows)), "tp", 0, 0, tiled=True
    )
    total = outs[0].astype(f32)
    moved = []
    for s in (6, 5, 7, 4, 2, 1, 3):
        moved.append(to_chip(outs[s], s // 4, s % 4))

    for value in moved:
        total = total + value.astype(f32)
    features = jnp.maximum(total + enc_bias, 0.0).astype(bf16)

    every = every.reshape(16, 4, rows).sum(axis=0)
    edit = jnp.zeros((rows, width), f32)
    own_quarter = clamp_ids // QUARTER
    for k in range(4):
        value = jnp.sum(jnp.where(own_quarter == my_quarter ^ k, clamp_values, 0.0), axis=1)
        bias = jnp.sum(held[k][:, 2 * width :].astype(f32), axis=1)
        now = jnp.maximum(every[k] + bias, 0.0).astype(bf16).astype(f32)
        delta = (value - now).astype(bf16).astype(f32)
        edit = edit + delta[:, None] * held[k][:, :width].astype(f32)
    resid_out = (resid_mid.astype(f32) + edit).astype(bf16)
    return (resid_out, features)


def solution(mesh):
    placed = (
        P("grp", "tp"),
        P("grp", "tp"),
        P(None, "grp", "tp", None, None),
        P(None, "grp", None, None),
        P("grp"),
        P("tp", None),
        P("tp", "grp"),
        P("grp"),
        P("grp", "tp"),
        P("grp", None),
        P("grp", None),
    )
    return jax.shard_map(
        per_device,
        mesh=mesh,
        in_specs=placed,
        out_specs=(P("grp", "tp"), P("tp", "grp")),
        check_vma=False,
    )
```

```python
import jax
import jax.numpy as jnp
from jax import lax
from jax.experimental import pallas as pl
from jax.experimental.pallas import tpu as pltpu
from jax.experimental import pallas as pl
from jax.experimental.pallas import tpu as pltpu
from jax.sharding import PartitionSpec as P

HEAD_DIM = 128
QUARTER = 8192


def tp_moves(move):
    return [(chip * 2 + core, move(chip, core)) for chip in range(8) for core in range(2)]


def grp_moves(move):
    return [(z * 2 + plane, move(z, plane)) for z in range(8) for plane in range(2)]


def swap_core(value):
    return lax.ppermute(value, "tp", tp_moves(lambda chip, core: chip * 2 + 1 - core))


def from_z(value, ahead):
    return lax.ppermute(
        value, "grp", grp_moves(lambda z, plane: (z - ahead) % 8 * 2 + plane)
    )


def chip_at(chip, dx, dy):
    return (chip // 4 + dx) % 2 * 4 + (chip + dy) % 4


def to_chip(value, dx, dy):
    return lax.ppermute(
        value, "tp", tp_moves(lambda chip, core: chip_at(chip, dx, dy) * 2 + core)
    )


def attend(queries, kv_cache, new_kv, lengths, kv_index):
    row_count = queries.shape[0]
    own_heads = queries.shape[1] // HEAD_DIM
    slot_count = kv_cache.shape[3]
    score_scale = HEAD_DIM ** (-0.5)
    query_heads = queries.reshape(row_count, own_heads, HEAD_DIM)
    cache_keys = kv_cache[0, :, 0]
    cache_values = kv_cache[1, :, 0]
    new_key = lax.dynamic_index_in_dim(new_kv[0], kv_index, 1, keepdims=False)
    new_value = lax.dynamic_index_in_dim(new_kv[1], kv_index, 1, keepdims=False)
    scores = (
        jnp.einsum("shd,spd->shp", query_heads, cache_keys, preferred_element_type=jnp.float32)
        * score_scale
    )
    new_score = (
        jnp.einsum("shd,sd->sh", query_heads, new_key, preferred_element_type=jnp.float32)
        * score_scale
    )
    slot_index = jnp.arange(slot_count, dtype=jnp.int32)
    is_valid = (slot_index[None, :] < lengths[:, None])[:, None, :]
    top_score = jnp.maximum(jnp.max(jnp.where(is_valid, scores, -jnp.inf), axis=-1), new_score)
    prob_cache = jnp.where(is_valid, jnp.exp(scores - top_score[..., None]), 0.0)
    new_prob = jnp.exp(new_score - top_score)
    total_weight = jnp.sum(prob_cache, axis=-1) + new_prob
    new_rounded = lax.optimization_barrier(new_prob.astype(jnp.bfloat16)).astype(jnp.float32)
    weighted = jnp.einsum(
        "shp,spd->shd",
        prob_cache.astype(jnp.bfloat16),
        cache_values,
        preferred_element_type=jnp.float32,
    )
    weighted = weighted + new_rounded[..., None] * new_value.astype(jnp.float32)[:, None, :]
    return (
        (weighted / total_weight[..., None])
        .astype(jnp.bfloat16)
        .reshape(row_count, own_heads * HEAD_DIM)
    )


def mm(a, b):
    return jnp.dot(a, b, preferred_element_type=jnp.float32)


def project_kernel(core_ref, mine_ref, other_ref, *refs):
    weight_refs, out_ref = refs[:4], refs[4]
    for i in range(2):
        out_ref[i] = (
            mm(mine_ref[...], weight_refs[i][...]) + mm(other_ref[...], weight_refs[2 + i][...])
        ).astype(out_ref.dtype)


def project(core, heads_mine, heads_other, w_mine, w_other, width):
    rows, depth = heads_mine.shape
    columns = [pl.BlockSpec((depth, width), lambda i, core_ref, e=e: (0, 4 * i + 2 * e + core_ref[0])) for e in range(2)]
    whole = pl.BlockSpec((rows, depth), lambda i, core_ref: (0, 0))
    return pl.pallas_call(
        project_kernel,
        grid_spec=pltpu.PrefetchScalarGridSpec(
            num_scalar_prefetch=1,
            grid=(4,),
            in_specs=[whole, whole] + columns + columns,
            out_specs=pl.BlockSpec((2, rows, width), lambda i, core_ref: (i, 0, 0)),
        ),
        out_shape=jax.ShapeDtypeStruct((8, rows, width), jnp.bfloat16),
        cost_estimate=pl.CostEstimate(
            flops=2 * rows * 2 * depth * 8 * width,
            bytes_accessed=2 * 2 * depth * 8 * width,
            transcendentals=0,
        ),
        name="project",
    )(core.reshape(1), heads_mine, heads_other, w_mine, w_mine, w_other, w_other)


def encode_kernel(place_ref, *refs):
    block_refs, (want_ref, bias_ref, w_mine_ref, w_other_ref) = refs[:8], refs[8:12]
    out_refs, now_ref = refs[12:20], refs[20]
    x_ref, held_ref, sems = refs[21:]
    step = pl.program_id(0)
    half, tile = w_mine_ref.shape
    rows = out_refs[0].shape[0]

    @pl.when(step == 0)
    def _():
        copies = [
            pltpu.make_async_copy(
                block_refs[k],
                x_ref.at[pl.ds(pl.multiple_of(place_ref[k] * rows, rows), rows), :],
                sems.at[k],
            )
            for k in range(8)
        ]
        for copy in copies:
            copy.start()
        held_ref[...] = jnp.zeros_like(held_ref)
        for copy in copies:
            copy.wait()

    part = mm(x_ref[:, :half], w_mine_ref[...]) + mm(x_ref[:, half:], w_other_ref[...])
    part = part.astype(jnp.bfloat16)
    for slot in range(8):
        out_refs[slot][...] = part[slot * rows : (slot + 1) * rows]
    lanes = held_ref.shape[1]
    want = want_ref[...] - step * tile
    for at in range(0, tile, lanes):
        piece = part[:, at : at + lanes].astype(jnp.float32) + bias_ref[:, at : at + lanes]
        column = lax.broadcasted_iota(jnp.int32, piece.shape, 1) + at
        held_ref[...] += jnp.where(column == want, piece, 0.0)

    @pl.when(step == pl.num_programs(0) - 1)
    def _():
        total = lax.dot_general(
            jnp.ones((8, lanes), jnp.float32),
            held_ref[...],
            (((1,), (1,)), ((), ())),
            precision=lax.Precision.HIGHEST,
            preferred_element_type=jnp.float32,
        )
        now_ref[...] = jnp.zeros_like(now_ref)
        for slot in range(8):
            now_ref[pl.ds(place_ref[8 + slot], 1), :] = total[:1, slot * rows : (slot + 1) * rows]


def encode(block, place, want, bias, w_mine, w_other):
    rows, depth = block[0].shape
    count = 8 * rows
    span = w_mine.shape[1]
    tile = 512
    return pl.pallas_call(
        encode_kernel,
        grid_spec=pltpu.PrefetchScalarGridSpec(
            num_scalar_prefetch=1,
            grid=(span // tile,),
            in_specs=[pl.BlockSpec(memory_space=pl.ANY)] * 8
            + [
                pl.BlockSpec((count, 1), lambda i, place: (0, 0)),
                pl.BlockSpec((1, tile), lambda i, place: (0, i)),
                pl.BlockSpec((depth // 2, tile), lambda i, place: (0, i)),
                pl.BlockSpec((depth // 2, tile), lambda i, place: (0, i)),
            ],
            out_specs=[pl.BlockSpec((rows, tile), lambda i, place: (0, i))] * 8
            + [pl.BlockSpec((16, rows), lambda i, place: (0, 0))],
            scratch_shapes=[
                pltpu.VMEM((count, depth), jnp.bfloat16),
                pltpu.VMEM((count, 128), jnp.float32),
                pltpu.SemaphoreType.DMA((8,)),
            ],
        ),
        out_shape=[jax.ShapeDtypeStruct((rows, span), jnp.bfloat16)] * 8
        + [jax.ShapeDtypeStruct((16, rows), jnp.float32)],
        cost_estimate=pl.CostEstimate(
            flops=2 * count * depth * span,
            bytes_accessed=2 * (depth * span + count * (depth + span)),
            transcendentals=0,
        ),
        name="encode",
    )(place, *block, want, bias, w_mine, w_other)


def per_device(
    resid_in,
    queries,
    kv_cache,
    new_kv,
    lengths,
    out_weight,
    enc_weight,
    enc_bias,
    dec_weight,
    clamp_ids,
    clamp_values,
):
    f32, bf16 = jnp.float32, jnp.bfloat16
    tp_rank, grp_rank = lax.axis_index("tp"), lax.axis_index("grp")
    chip, core = tp_rank // 2, tp_rank % 2
    z, plane = grp_rank // 2, grp_rank % 2
    rows, width = resid_in.shape
    span = enc_weight.shape[1]
    my_quarter, parity = z // 2, z % 2

    ids = lax.all_to_all(
        jnp.broadcast_to(clamp_ids[:, 0].reshape(1, 1, rows), (16, 1, rows)), "grp", 0, 0, tiled=True
    ).reshape(16, rows)
    out_other = swap_core(out_weight)
    enc_other = swap_core(enc_weight)

    heads_mine = attend(queries, kv_cache, new_kv, lengths, tp_rank // 4)
    heads_other = swap_core(heads_mine)
    part = project(core, heads_mine, heads_other, out_weight, out_other, width)
    groups = [[c + 2 * i for i in range(8)] for c in range(2)]
    arrived = lax.all_to_all(part, "tp", 0, 0, axis_index_groups=groups, tiled=True)
    resid_mid = (resid_in.astype(f32) + jnp.sum(arrived.astype(f32), axis=0)).astype(bf16)

    want = ids % QUARTER + my_quarter * QUARTER - grp_rank * span
    ordered = want.reshape(4, 2, 2, rows).transpose(1, 2, 0, 3)
    ordered = jnp.where(parity == 1, ordered, ordered[::-1])
    ordered = jnp.where(plane == 1, ordered, ordered[:, ::-1]).reshape(16 * rows)
    hits = (ordered[:, None] == jnp.arange(span, dtype=jnp.int32)[None, :]).astype(bf16)
    found = mm(hits, dec_weight).astype(bf16)

    mid_other = swap_core(resid_mid)
    both = jnp.concatenate([resid_mid, mid_other], axis=1)
    cross = [
        (t * 16 + z_ * 2 + t % 2, t * 16 + z_ * 2 + 1 - t % 2) for t in range(16) for z_ in range(8)
    ]
    crossed = lax.ppermute(both, ("tp", "grp"), cross)
    near = lax.ppermute(found[: 8 * rows], "grp", grp_moves(lambda z_, s: (z_ ^ 1) * 2 + s))
    block = [None] * 8
    block[0] = jnp.where(core == plane, both, crossed)
    for k, source, step in (
        (1, 0, 1), (7, 0, 7), (2, 0, 2), (6, 0, 6),
        (3, 2, 1), (5, 6, 7), (4, 2, 2),
    ):
        block[k] = from_z(block[source], step)
    found = found[8 * rows :] + near
    near = lax.ppermute(found[: 4 * rows], "grp", grp_moves(lambda z_, s: z_ * 2 + 1 - s))
    found = (found[4 * rows :] + near).reshape(4, rows, width)
    dec_rows = [lax.dynamic_index_in_dim(found, my_quarter, 0, keepdims=False)]
    for k in (1, 2, 3):
        give = lax.dynamic_index_in_dim(found, (my_quarter + k) % 4, 0, keepdims=False)
        dec_rows.append(from_z(give, -2 * k))

    target = [chip_at(chip, s // 4, s % 4) for s in range(8)]
    ahead = (jnp.arange(8, dtype=jnp.int32) + z) % 8
    slot = (ahead // 4 + chip // 4) % 2 * 4 + (ahead - chip) % 4
    mine = lax.dynamic_index_in_dim(want.reshape(8, 2, rows), core, 1, keepdims=False)
    slots = jnp.concatenate([lax.dynamic_index_in_dim(mine, t, 0, keepdims=False) for t in target])
    bias = jnp.where(chip == 0, enc_bias, 0.0).reshape(1, span)
    each = jnp.arange(8, dtype=jnp.int32)
    goal = ((chip // 4 + each // 4) % 2 * 4 + (chip + each) % 4) * 2 + core
    outs = encode(
        block, jnp.concatenate([slot, goal]), slots.reshape(8 * rows, 1), bias, enc_weight, enc_other
    )

    relayed = to_chip(outs[6], 0, 3)
    seven = outs[7] + relayed
    relayed = to_chip(outs[2], 0, 1)
    one = outs[1] + relayed
    moved = []
    for value, s in ((outs[4], 4), (outs[5], 5), (outs[3], 3), (seven, 7), (one, 1)):
        moved.append(to_chip(value, s // 4, s % 4))

    held = lax.all_to_all(outs[8].reshape(16, 1, rows), "grp", 0, 0, tiled=True)
    held = held.reshape(4, 4, rows).sum(axis=1)
    every = lax.all_to_all(
        jnp.broadcast_to(held[None], (16, 4, rows)), "tp", 0, 0, tiled=True
    )
    total = outs[0].astype(f32)
    for value in moved:
        total = total + value.astype(f32)
    features = jnp.maximum(total + enc_bias, 0.0).astype(bf16)

    every = every.reshape(16, 4, rows).sum(axis=0)
    every = jnp.maximum(every, 0.0).astype(bf16).astype(f32)
    edit = jnp.zeros((rows, width), f32)
    own_quarter = clamp_ids // QUARTER
    for k in range(4):
        q = (my_quarter - k) % 4
        value = jnp.sum(jnp.where(own_quarter == q, clamp_values, 0.0), axis=1)
        delta = (value - lax.dynamic_index_in_dim(every, q, 0, keepdims=False)).astype(bf16)
        edit = edit + delta.astype(f32)[:, None] * dec_rows[k].astype(f32)
    resid_out = (resid_mid.astype(f32) + edit).astype(bf16)
    return (resid_out, features)


def solution(mesh):
    placed = (
        P("grp", "tp"),
        P("grp", "tp"),
        P(None, "grp", "tp", None, None),
        P(None, "grp", None, None),
        P("grp"),
        P("tp", None),
        P("tp", "grp"),
        P("grp"),
        P("grp", "tp"),
        P("grp", None),
        P("grp", None),
    )
    return jax.shard_map(
        per_device,
        mesh=mesh,
        in_specs=placed,
        out_specs=(P("grp", "tp"), P("tp", "grp")),
        check_vma=False,
    )
```

```python
import jax
import jax.numpy as jnp
from jax import lax
from jax.experimental import pallas as pl
from jax.experimental.pallas import tpu as pltpu
from jax.experimental import pallas as pl
from jax.experimental.pallas import tpu as pltpu
from jax.sharding import PartitionSpec as P

HEAD_DIM = 128
QUARTER = 8192


def tp_moves(move):
    return [(chip * 2 + core, move(chip, core)) for chip in range(8) for core in range(2)]


def grp_moves(move):
    return [(z * 2 + plane, move(z, plane)) for z in range(8) for plane in range(2)]


def swap_core(value):
    return lax.ppermute(value, "tp", tp_moves(lambda chip, core: chip * 2 + 1 - core))


def from_z(value, ahead):
    return lax.ppermute(
        value, "grp", grp_moves(lambda z, plane: (z - ahead) % 8 * 2 + plane)
    )


def flip_z(value, k):
    return lax.ppermute(value, "grp", grp_moves(lambda z, plane: (z ^ k) * 2 + plane))


def flip_plane(value):
    return lax.ppermute(value, "grp", grp_moves(lambda z, plane: z * 2 + 1 - plane))


def chip_at(chip, dx, dy):
    return (chip // 4 + dx) % 2 * 4 + (chip + dy) % 4


def to_chip(value, dx, dy):
    return lax.ppermute(
        value, "tp", tp_moves(lambda chip, core: chip_at(chip, dx, dy) * 2 + core)
    )


def attend(queries, kv_cache, new_kv, lengths, kv_index):
    row_count = queries.shape[0]
    own_heads = queries.shape[1] // HEAD_DIM
    slot_count = kv_cache.shape[3]
    score_scale = HEAD_DIM ** (-0.5)
    query_heads = queries.reshape(row_count, own_heads, HEAD_DIM)
    cache_keys = kv_cache[0, :, 0]
    cache_values = kv_cache[1, :, 0]
    new_key = lax.dynamic_index_in_dim(new_kv[0], kv_index, 1, keepdims=False)
    new_value = lax.dynamic_index_in_dim(new_kv[1], kv_index, 1, keepdims=False)
    scores = (
        jnp.einsum("shd,spd->shp", query_heads, cache_keys, preferred_element_type=jnp.float32)
        * score_scale
    )
    new_score = (
        jnp.einsum("shd,sd->sh", query_heads, new_key, preferred_element_type=jnp.float32)
        * score_scale
    )
    slot_index = jnp.arange(slot_count, dtype=jnp.int32)
    is_valid = (slot_index[None, :] < lengths[:, None])[:, None, :]
    top_score = jnp.maximum(jnp.max(jnp.where(is_valid, scores, -jnp.inf), axis=-1), new_score)
    prob_cache = jnp.where(is_valid, jnp.exp(scores - top_score[..., None]), 0.0)
    new_prob = jnp.exp(new_score - top_score)
    total_weight = jnp.sum(prob_cache, axis=-1) + new_prob
    new_rounded = lax.optimization_barrier(new_prob.astype(jnp.bfloat16)).astype(jnp.float32)
    weighted = jnp.einsum(
        "shp,spd->shd",
        prob_cache.astype(jnp.bfloat16),
        cache_values,
        preferred_element_type=jnp.float32,
    )
    weighted = weighted + new_rounded[..., None] * new_value.astype(jnp.float32)[:, None, :]
    return (
        (weighted / total_weight[..., None])
        .astype(jnp.bfloat16)
        .reshape(row_count, own_heads * HEAD_DIM)
    )


def mm(a, b):
    return jnp.dot(a, b, preferred_element_type=jnp.float32)


def project_kernel(core_ref, mine_ref, other_ref, *refs):
    weight_refs, out_ref = refs[:4], refs[4]
    for i in range(2):
        out_ref[i] = (
            mm(mine_ref[...], weight_refs[i][...]) + mm(other_ref[...], weight_refs[2 + i][...])
        ).astype(out_ref.dtype)


def project(core, heads_mine, heads_other, w_mine, w_other, width):
    rows, depth = heads_mine.shape
    columns = [pl.BlockSpec((depth, width), lambda i, core_ref, e=e: (0, 4 * i + 2 * e + core_ref[0])) for e in range(2)]
    whole = pl.BlockSpec((rows, depth), lambda i, core_ref: (0, 0))
    return pl.pallas_call(
        project_kernel,
        grid_spec=pltpu.PrefetchScalarGridSpec(
            num_scalar_prefetch=1,
            grid=(4,),
            in_specs=[whole, whole] + columns + columns,
            out_specs=pl.BlockSpec((2, rows, width), lambda i, core_ref: (i, 0, 0)),
        ),
        out_shape=jax.ShapeDtypeStruct((8, rows, width), jnp.bfloat16),
        cost_estimate=pl.CostEstimate(
            flops=2 * rows * 2 * depth * 8 * width,
            bytes_accessed=2 * 2 * depth * 8 * width,
            transcendentals=0,
        ),
        name="project",
    )(core.reshape(1), heads_mine, heads_other, w_mine, w_mine, w_other, w_other)


def encode_kernel(place_ref, *refs):
    block_refs, (bias_ref, w_mine_ref, w_other_ref) = refs[:8], refs[8:11]
    out_refs, table_ref = refs[11:19], refs[19]
    x_ref, held_ref, sems = refs[20:]
    f32 = jnp.float32
    step = pl.program_id(0)
    half, tile = w_mine_ref.shape
    rows = out_refs[0].shape[0]
    lanes = held_ref.shape[1]

    @pl.when(step == 0)
    def _():
        copies = [
            pltpu.make_async_copy(
                block_refs[k],
                x_ref.at[pl.ds(pl.multiple_of(place_ref[k] * rows, rows), rows), :],
                sems.at[k],
            )
            for k in range(8)
        ]
        for copy in copies:
            copy.start()
        held_ref[...] = jnp.zeros_like(held_ref)
        for copy in copies:
            copy.wait()

    part = mm(x_ref[:, :half], w_mine_ref[...]) + mm(x_ref[:, half : 2 * half], w_other_ref[...])
    part = part.astype(jnp.bfloat16)
    for slot in range(8):
        out_refs[slot][...] = part[slot * rows : (slot + 1) * rows]
    first_id = (
        x_ref[:, 2 * half : 2 * half + 1].astype(f32) * 256.0
        + x_ref[:, 2 * half + 1 : 2 * half + 2].astype(f32)
    ).astype(jnp.int32)
    want = (first_id & (QUARTER - 1)) - place_ref[16] - step * tile
    for at in range(0, tile, lanes):
        piece = part[:, at : at + lanes].astype(f32) + bias_ref[:, at : at + lanes]
        column = lax.broadcasted_iota(jnp.int32, piece.shape, 1) + at
        held_ref[...] += jnp.where(column == want, piece, 0.0)

    @pl.when(step == pl.num_programs(0) - 1)
    def _():
        over_lanes = lambda a, b, precision: lax.dot_general(
            a, b, (((1,), (1,)), ((), ())), precision=precision, preferred_element_type=f32
        )
        now = over_lanes(jnp.ones((8, lanes), f32), held_ref[...], lax.Precision.HIGHEST)[:1]
        shape = (16, lanes)
        pick = lax.broadcasted_iota(jnp.int32, shape, 0) == lax.broadcasted_iota(jnp.int32, shape, 1)
        pick = pick.astype(f32).astype(jnp.bfloat16)
        extra = over_lanes(pick, x_ref[:, 2 * half :], None)
        ids = (extra[0:1] * 256.0 + extra[1:2]).astype(jnp.int32)
        local = ((ids & (QUARTER - 1)) - place_ref[16]).astype(f32)
        index = (place_ref[17] - (ids >> 13)) & 3
        value = jnp.zeros_like(local)
        for c in range(4):
            whole = extra[2 + 3 * c : 3 + 3 * c] + extra[3 + 3 * c : 4 + 3 * c]
            value += jnp.where(index == c, whole + extra[4 + 3 * c : 5 + 3 * c], 0.0)
        for slot in range(8):
            for at, source in enumerate((now, local, value)):
                table_ref[pl.ds(8 * at + place_ref[8 + slot], 1), :] = source[
                    :, slot * rows : (slot + 1) * rows
                ]


def encode(block, place, bias, w_mine, w_other):
    rows, depth = block[0].shape
    count = 8 * rows
    half, span = w_mine.shape
    tile = 512
    return pl.pallas_call(
        encode_kernel,
        grid_spec=pltpu.PrefetchScalarGridSpec(
            num_scalar_prefetch=1,
            grid=(span // tile,),
            in_specs=[pl.BlockSpec(memory_space=pl.ANY)] * 8
            + [
                pl.BlockSpec((1, tile), lambda i, place: (0, i)),
                pl.BlockSpec((half, tile), lambda i, place: (0, i)),
                pl.BlockSpec((half, tile), lambda i, place: (0, i)),
            ],
            out_specs=[pl.BlockSpec((rows, tile), lambda i, place: (0, i))] * 8
            + [pl.BlockSpec((24, rows), lambda i, place: (0, 0))],
            scratch_shapes=[
                pltpu.VMEM((count, depth), jnp.bfloat16),
                pltpu.VMEM((count, 128), jnp.float32),
                pltpu.SemaphoreType.DMA((8,)),
            ],
        ),
        out_shape=[jax.ShapeDtypeStruct((rows, span), jnp.bfloat16)] * 8
        + [jax.ShapeDtypeStruct((24, rows), jnp.float32)],
        cost_estimate=pl.CostEstimate(
            flops=4 * count * half * span,
            bytes_accessed=2 * (2 * half * span + count * (depth + span)),
            transcendentals=0,
        ),
        name="encode",
    )(place, *block, bias, w_mine, w_other)


def per_device(
    resid_in,
    queries,
    kv_cache,
    new_kv,
    lengths,
    out_weight,
    enc_weight,
    enc_bias,
    dec_weight,
    clamp_ids,
    clamp_values,
):
    f32, bf16 = jnp.float32, jnp.bfloat16
    tp_rank, grp_rank = lax.axis_index("tp"), lax.axis_index("grp")
    chip, core = tp_rank // 2, tp_rank % 2
    z, plane = grp_rank // 2, grp_rank % 2
    rows, width = resid_in.shape
    span = enc_weight.shape[1]
    my_quarter = z // 2

    out_other = swap_core(out_weight)
    enc_other = swap_core(enc_weight)

    heads_mine = attend(queries, kv_cache, new_kv, lengths, tp_rank // 4)
    heads_other = swap_core(heads_mine)
    part = project(core, heads_mine, heads_other, out_weight, out_other, width)
    groups = [[c + 2 * i for i in range(8)] for c in range(2)]
    arrived = lax.all_to_all(part, "tp", 0, 0, axis_index_groups=groups, tiled=True)
    resid_mid = (resid_in.astype(f32) + jnp.sum(arrived.astype(f32), axis=0)).astype(bf16)

    mid_other = swap_core(resid_mid)
    coarse = lambda value: lax.reduce_precision(value, 8, 7)
    high = coarse(clamp_values)
    middle = coarse(clamp_values - high)
    parts = jnp.stack([high, middle, clamp_values - high - middle], axis=2).reshape(rows, 12)
    first_id = clamp_ids[:, :1]
    id_parts = jnp.concatenate([first_id // 256, first_id % 256], axis=1).astype(f32)
    extra = jnp.concatenate([id_parts, parts, jnp.zeros((rows, 114), f32)], axis=1).astype(bf16)
    both = jnp.concatenate([resid_mid, mid_other, extra], axis=1)
    cross = [
        (t * 16 + z_ * 2 + t % 2, t * 16 + z_ * 2 + 1 - t % 2) for t in range(16) for z_ in range(8)
    ]
    crossed = lax.ppermute(both, ("tp", "grp"), cross)
    block = [None] * 8
    block[0] = jnp.where(core == plane, both, crossed)
    for k, source, step in (
        (1, 0, 1), (7, 0, 7), (2, 0, 2), (6, 0, 6),
        (3, 2, 1), (5, 6, 7), (4, 2, 2),
    ):
        block[k] = from_z(block[source], step)
    ahead = (jnp.arange(8, dtype=jnp.int32) + z) % 8
    slot = (ahead // 4 + chip // 4) % 2 * 4 + (ahead - chip) % 4
    bias = jnp.where(chip == 0, enc_bias, 0.0).reshape(1, span)
    each = jnp.arange(8, dtype=jnp.int32)
    goal = ((chip // 4 + each // 4) % 2 * 4 + (chip + each) % 4 - z) % 8
    others = jnp.stack([grp_rank % 4 * span, my_quarter])
    outs = encode(
        block, jnp.concatenate([slot, goal, others]), bias, enc_weight, enc_other
    )

    table = lax.all_to_all(
        jnp.broadcast_to(outs[8][None], (16, 24, rows)), "tp", 0, 0, tiled=True
    ).reshape(8, 2, 24, rows)
    now = jnp.maximum(table[:, :, :8].sum(axis=0), 0.0)
    now = lax.reduce_precision(now, 8, 7)
    want, delta = table[0, :, 8:16], table[0, :, 16:] - now

    def arrange(value):
        value = jnp.where(plane == 1, value, value[::-1])
        odd = value[:, 1::2]
        odd = jnp.where(z % 2 == 0, odd, jnp.concatenate([odd[:, 3:], odd[:, :3]], axis=1))
        return odd.reshape(8 * rows), value[:, 0::2].reshape(8 * rows)

    def decode(want, delta):
        column = jnp.arange(span, dtype=jnp.int32)[None, :]
        hits = jnp.where(column == want.astype(jnp.int32)[:, None], delta[:, None], 0.0)
        return mm(hits.astype(bf16), dec_weight)

    want_give, want_keep = arrange(want)
    delta_give, delta_keep = arrange(delta)
    give = decode(want_give, delta_give).astype(bf16)
    near = flip_z(give, 1)
    keep = decode(want_keep, delta_keep).astype(bf16)
    first, last = slice(0, 4 * rows), slice(4 * rows, 8 * rows)
    near_2 = flip_plane(keep[first] + near[first])
    found = keep[last] + near[last] + near_2
    edit = found[:rows].astype(f32)
    edits = []
    for k in (1, 2, 3):
        edits.append(from_z(found[k * rows : (k + 1) * rows], -2 * k))

    relayed = to_chip(outs[6], 0, 3)
    seven = outs[7] + relayed
    relayed = to_chip(outs[2], 0, 1)
    one = outs[1] + relayed
    moved = []
    for value, s in ((outs[4], 4), (outs[5], 5), (outs[3], 3), (seven, 7), (one, 1)):
        moved.append(to_chip(value, s // 4, s % 4))

    total = outs[0].astype(f32)
    for value in moved:
        total = total + value.astype(f32)
    features = jnp.maximum(total + enc_bias, 0.0).astype(bf16)

    for value in edits:
        edit = edit + value.astype(f32)
    resid_out = (resid_mid.astype(f32) + edit).astype(bf16)
    return (resid_out, features)


def solution(mesh):
    placed = (
        P("grp", "tp"),
        P("grp", "tp"),
        P(None, "grp", "tp", None, None),
        P(None, "grp", None, None),
        P("grp"),
        P("tp", None),
        P("tp", "grp"),
        P("grp"),
        P("grp", "tp"),
        P("grp", None),
        P("grp", None),
    )
    return jax.shard_map(
        per_device,
        mesh=mesh,
        in_specs=placed,
        out_specs=(P("grp", "tp"), P("tp", "grp")),
        check_vma=False,
    )
```

```python
import jax
import jax.numpy as jnp
from jax import lax
from jax.experimental import pallas as pl
from jax.experimental.pallas import tpu as pltpu
from jax.experimental import pallas as pl
from jax.experimental.pallas import tpu as pltpu
from jax.sharding import PartitionSpec as P

HEAD_DIM = 128
QUARTER = 8192


def tp_moves(move):
    return [(chip * 2 + core, move(chip, core)) for chip in range(8) for core in range(2)]


def grp_moves(move):
    return [(z * 2 + plane, move(z, plane)) for z in range(8) for plane in range(2)]


def swap_core(value):
    return lax.ppermute(value, "tp", tp_moves(lambda chip, core: chip * 2 + 1 - core))


def from_z(value, ahead):
    return lax.ppermute(
        value, "grp", grp_moves(lambda z, plane: (z - ahead) % 8 * 2 + plane)
    )


def flip_z(value, k):
    return lax.ppermute(value, "grp", grp_moves(lambda z, plane: (z ^ k) * 2 + plane))


def flip_plane(value):
    return lax.ppermute(value, "grp", grp_moves(lambda z, plane: z * 2 + 1 - plane))


def chip_at(chip, dx, dy):
    return (chip // 4 + dx) % 2 * 4 + (chip + dy) % 4


def to_chip(value, dx, dy):
    return lax.ppermute(
        value, "tp", tp_moves(lambda chip, core: chip_at(chip, dx, dy) * 2 + core)
    )


def attend(queries, kv_cache, new_kv, lengths, kv_index):
    row_count = queries.shape[0]
    own_heads = queries.shape[1] // HEAD_DIM
    slot_count = kv_cache.shape[3]
    score_scale = HEAD_DIM ** (-0.5)
    query_heads = queries.reshape(row_count, own_heads, HEAD_DIM)
    cache_keys = kv_cache[0, :, 0]
    cache_values = kv_cache[1, :, 0]
    new_key = lax.dynamic_index_in_dim(new_kv[0], kv_index, 1, keepdims=False)
    new_value = lax.dynamic_index_in_dim(new_kv[1], kv_index, 1, keepdims=False)
    scores = (
        jnp.einsum("shd,spd->shp", query_heads, cache_keys, preferred_element_type=jnp.float32)
        * score_scale
    )
    new_score = (
        jnp.einsum("shd,sd->sh", query_heads, new_key, preferred_element_type=jnp.float32)
        * score_scale
    )
    slot_index = jnp.arange(slot_count, dtype=jnp.int32)
    is_valid = (slot_index[None, :] < lengths[:, None])[:, None, :]
    top_score = jnp.maximum(jnp.max(jnp.where(is_valid, scores, -jnp.inf), axis=-1), new_score)
    prob_cache = jnp.where(is_valid, jnp.exp(scores - top_score[..., None]), 0.0)
    new_prob = jnp.exp(new_score - top_score)
    total_weight = jnp.sum(prob_cache, axis=-1) + new_prob
    new_rounded = lax.optimization_barrier(new_prob.astype(jnp.bfloat16)).astype(jnp.float32)
    weighted = jnp.einsum(
        "shp,spd->shd",
        prob_cache.astype(jnp.bfloat16),
        cache_values,
        preferred_element_type=jnp.float32,
    )
    weighted = weighted + new_rounded[..., None] * new_value.astype(jnp.float32)[:, None, :]
    return (
        (weighted / total_weight[..., None])
        .astype(jnp.bfloat16)
        .reshape(row_count, own_heads * HEAD_DIM)
    )


def mm(a, b):
    return jnp.dot(a, b, preferred_element_type=jnp.float32)


def project_kernel(core_ref, mine_ref, other_ref, *refs):
    weight_refs, out_ref = refs[:4], refs[4]
    for i in range(2):
        out_ref[i] = (
            mm(mine_ref[...], weight_refs[i][...]) + mm(other_ref[...], weight_refs[2 + i][...])
        ).astype(out_ref.dtype)


def project(core, heads_mine, heads_other, w_mine, w_other, width):
    rows, depth = heads_mine.shape
    columns = [pl.BlockSpec((depth, width), lambda i, core_ref, e=e: (0, 4 * i + 2 * e + core_ref[0])) for e in range(2)]
    whole = pl.BlockSpec((rows, depth), lambda i, core_ref: (0, 0))
    return pl.pallas_call(
        project_kernel,
        grid_spec=pltpu.PrefetchScalarGridSpec(
            num_scalar_prefetch=1,
            grid=(4,),
            in_specs=[whole, whole] + columns + columns,
            out_specs=pl.BlockSpec((2, rows, width), lambda i, core_ref: (i, 0, 0)),
        ),
        out_shape=jax.ShapeDtypeStruct((8, rows, width), jnp.bfloat16),
        cost_estimate=pl.CostEstimate(
            flops=2 * rows * 2 * depth * 8 * width,
            bytes_accessed=2 * 2 * depth * 8 * width,
            transcendentals=0,
        ),
        name="project",
    )(core.reshape(1), heads_mine, heads_other, w_mine, w_mine, w_other, w_other)


def encode_kernel(place_ref, *refs):
    block_refs, (bias_ref, w_mine_ref, w_other_ref) = refs[:8], refs[8:11]
    out_refs, table_ref = refs[11:19], refs[19]
    x_ref, held_ref, row_ref, sems = refs[20:]
    f32 = jnp.float32
    step = pl.program_id(0)
    half, tile = w_mine_ref.shape
    rows = out_refs[0].shape[0]
    lanes = held_ref.shape[1]

    @pl.when(step == 0)
    def _():
        copies = [
            pltpu.make_async_copy(
                block_refs[k],
                x_ref.at[pl.ds(pl.multiple_of(place_ref[k] * rows, rows), rows), :],
                sems.at[k],
            )
            for k in range(8)
        ]
        for copy in copies:
            copy.start()
        held_ref[...] = jnp.zeros_like(held_ref)
        for copy in copies:
            copy.wait()

    part = mm(x_ref[:, :half], w_mine_ref[...]) + mm(x_ref[:, half : 2 * half], w_other_ref[...])
    part = part.astype(jnp.bfloat16)
    for slot in range(8):
        out_refs[slot][...] = part[slot * rows : (slot + 1) * rows]
    first_id = (
        x_ref[:, 2 * half : 2 * half + 1].astype(f32) * 256.0
        + x_ref[:, 2 * half + 1 : 2 * half + 2].astype(f32)
    ).astype(jnp.int32)
    want = (first_id & (QUARTER - 1)) - place_ref[16] - step * tile
    for at in range(0, tile, lanes):
        piece = part[:, at : at + lanes].astype(f32) + bias_ref[:, at : at + lanes]
        column = lax.broadcasted_iota(jnp.int32, piece.shape, 1) + at
        held_ref[...] += jnp.where(column == want, piece, 0.0)

    @pl.when(step == pl.num_programs(0) - 1)
    def _():
        over_lanes = lambda a, b, precision: lax.dot_general(
            a, b, (((1,), (1,)), ((), ())), precision=precision, preferred_element_type=f32
        )
        now = over_lanes(jnp.ones((8, lanes), f32), held_ref[...], lax.Precision.HIGHEST)[:1]
        shape = (16, lanes)
        pick = lax.broadcasted_iota(jnp.int32, shape, 0) == lax.broadcasted_iota(jnp.int32, shape, 1)
        pick = pick.astype(f32).astype(jnp.bfloat16)
        extra = over_lanes(pick, x_ref[:, 2 * half :], None)
        ids = (extra[0:1] * 256.0 + extra[1:2]).astype(jnp.int32)
        local = ((ids & (QUARTER - 1)) - place_ref[16]).astype(f32)
        index = (place_ref[17] - (ids >> 13)) & 3
        value = jnp.zeros_like(local)
        for c in range(4):
            whole = extra[2 + 3 * c : 3 + 3 * c] + extra[3 + 3 * c : 4 + 3 * c]
            value += jnp.where(index == c, whole + extra[4 + 3 * c : 5 + 3 * c], 0.0)
        row_ref[...] = jnp.zeros_like(row_ref)
        for slot in range(8):
            for at, source in enumerate((now, local, value)):
                row_ref[pl.ds(8 * at + place_ref[8 + slot], 1), :rows] = source[
                    :, slot * rows : (slot + 1) * rows
                ]
        for i in range(16):
            table_ref[i] = row_ref[...]


def encode(block, place, bias, w_mine, w_other):
    rows, depth = block[0].shape
    count = 8 * rows
    half, span = w_mine.shape
    tile = 512
    return pl.pallas_call(
        encode_kernel,
        grid_spec=pltpu.PrefetchScalarGridSpec(
            num_scalar_prefetch=1,
            grid=(span // tile,),
            in_specs=[pl.BlockSpec(memory_space=pl.ANY)] * 8
            + [
                pl.BlockSpec((1, tile), lambda i, place: (0, i)),
                pl.BlockSpec((half, tile), lambda i, place: (0, i)),
                pl.BlockSpec((half, tile), lambda i, place: (0, i)),
            ],
            out_specs=[pl.BlockSpec((rows, tile), lambda i, place: (0, i))] * 8
            + [pl.BlockSpec((16, 24, 128), lambda i, place: (0, 0, 0))],
            scratch_shapes=[
                pltpu.VMEM((count, depth), jnp.bfloat16),
                pltpu.VMEM((count, 128), jnp.float32),
                pltpu.VMEM((24, 128), jnp.float32),
                pltpu.SemaphoreType.DMA((8,)),
            ],
        ),
        out_shape=[jax.ShapeDtypeStruct((rows, span), jnp.bfloat16)] * 8
        + [jax.ShapeDtypeStruct((16, 24, 128), jnp.float32)],
        cost_estimate=pl.CostEstimate(
            flops=4 * count * half * span,
            bytes_accessed=2 * (2 * half * span + count * (depth + span)),
            transcendentals=0,
        ),
        name="encode",
    )(place, *block, bias, w_mine, w_other)


def per_device(
    resid_in,
    queries,
    kv_cache,
    new_kv,
    lengths,
    out_weight,
    enc_weight,
    enc_bias,
    dec_weight,
    clamp_ids,
    clamp_values,
):
    f32, bf16 = jnp.float32, jnp.bfloat16
    tp_rank, grp_rank = lax.axis_index("tp"), lax.axis_index("grp")
    chip, core = tp_rank // 2, tp_rank % 2
    z, plane = grp_rank // 2, grp_rank % 2
    rows, width = resid_in.shape
    span = enc_weight.shape[1]
    my_quarter = z // 2

    out_other = swap_core(out_weight)
    enc_other = swap_core(enc_weight)

    heads_mine = attend(queries, kv_cache, new_kv, lengths, tp_rank // 4)
    heads_other = swap_core(heads_mine)
    part = project(core, heads_mine, heads_other, out_weight, out_other, width)
    groups = [[c + 2 * i for i in range(8)] for c in range(2)]
    arrived = lax.all_to_all(part, "tp", 0, 0, axis_index_groups=groups, tiled=True)
    resid_mid = (resid_in.astype(f32) + jnp.sum(arrived.astype(f32), axis=0)).astype(bf16)

    mid_other = swap_core(resid_mid)
    coarse = lambda value: lax.reduce_precision(value, 8, 7)
    high = coarse(clamp_values)
    middle = coarse(clamp_values - high)
    parts = jnp.stack([high, middle, clamp_values - high - middle], axis=2).reshape(rows, 12)
    first_id = clamp_ids[:, :1]
    id_parts = jnp.concatenate([first_id // 256, first_id % 256], axis=1).astype(f32)
    extra = jnp.concatenate([id_parts, parts, jnp.zeros((rows, 114), f32)], axis=1).astype(bf16)
    both = jnp.concatenate([resid_mid, mid_other, extra], axis=1)
    cross = [
        (t * 16 + z_ * 2 + t % 2, t * 16 + z_ * 2 + 1 - t % 2) for t in range(16) for z_ in range(8)
    ]
    crossed = lax.ppermute(both, ("tp", "grp"), cross)
    block = [None] * 8
    block[0] = jnp.where(core == plane, both, crossed)
    for k, source, step in (
        (1, 0, 1), (7, 0, 7), (2, 0, 2), (6, 0, 6),
        (3, 2, 1), (5, 6, 7), (4, 2, 2),
    ):
        block[k] = from_z(block[source], step)
    ahead = (jnp.arange(8, dtype=jnp.int32) + z) % 8
    slot = (ahead // 4 + chip // 4) % 2 * 4 + (ahead - chip) % 4
    bias = jnp.where(chip == 0, enc_bias, 0.0).reshape(1, span)
    each = jnp.arange(8, dtype=jnp.int32)
    goal = ((chip // 4 + each // 4) % 2 * 4 + (chip + each) % 4 - z) % 8
    others = jnp.stack([grp_rank % 4 * span, my_quarter])
    outs = encode(
        block, jnp.concatenate([slot, goal, others]), bias, enc_weight, enc_other
    )

    table = lax.all_to_all(outs[8], "tp", 0, 0, tiled=True)
    table = table[:, :, :rows].reshape(8, 2, 24, rows)
    now = jnp.maximum(table[:, :, :8].sum(axis=0), 0.0)
    now = lax.reduce_precision(now, 8, 7)
    want, delta = table[0, :, 8:16], table[0, :, 16:] - now

    def arrange(value):
        value = jnp.where(plane == 1, value, value[::-1])
        odd = value[:, 1::2]
        odd = jnp.where(z % 2 == 0, odd, jnp.concatenate([odd[:, 3:], odd[:, :3]], axis=1))
        return odd, value[:, 0::2]

    half = width // 2

    def decode(want, delta, columns):
        column = jnp.arange(span, dtype=jnp.int32)[None, :]
        hits = jnp.where(
            column == want.reshape(8 * rows).astype(jnp.int32)[:, None],
            delta.reshape(8 * rows)[:, None],
            0.0,
        )
        return mm(hits.astype(bf16), dec_weight[:, columns]).astype(bf16)

    want, delta = arrange(want), arrange(delta)
    across = lambda pair, at: jnp.stack([pair[0][at], pair[1][at]])
    left, right = slice(0, half), slice(half, width)
    give_z = decode(want[0], delta[0], left)
    near_z = flip_z(give_z, 1)
    give_p = decode(across(want, 0), across(delta, 0), right)
    near_p = flip_plane(give_p)
    keep_z = decode(want[1], delta[1], left)
    keep_p = decode(across(want, 1), across(delta, 1), right)
    first, last = slice(0, 4 * rows), slice(4 * rows, 8 * rows)
    near_pz = flip_z(keep_p[first] + near_p[first], 1)
    near_zp = flip_plane(keep_z[first] + near_z[first])
    found = jnp.concatenate(
        [keep_z[last] + near_z[last] + near_zp, keep_p[last] + near_p[last] + near_pz], axis=1
    )
    edit = found[:rows].astype(f32)
    edits = []
    for k in (1, 2, 3):
        edits.append(from_z(found[k * rows : (k + 1) * rows], -2 * k))

    relayed = to_chip(outs[6], 0, 3)
    seven = outs[7] + relayed
    relayed = to_chip(outs[2], 0, 1)
    one = outs[1] + relayed
    moved = []
    for value, s in ((outs[4], 4), (outs[5], 5), (outs[3], 3), (seven, 7), (one, 1)):
        moved.append(to_chip(value, s // 4, s % 4))

    total = outs[0].astype(f32)
    for value in moved:
        total = total + value.astype(f32)
    features = jnp.maximum(total + enc_bias, 0.0).astype(bf16)

    for value in edits:
        edit = edit + value.astype(f32)
    resid_out = (resid_mid.astype(f32) + edit).astype(bf16)
    return (resid_out, features)


def solution(mesh):
    placed = (
        P("grp", "tp"),
        P("grp", "tp"),
        P(None, "grp", "tp", None, None),
        P(None, "grp", None, None),
        P("grp"),
        P("tp", None),
        P("tp", "grp"),
        P("grp"),
        P("grp", "tp"),
        P("grp", None),
        P("grp", None),
    )
    return jax.shard_map(
        per_device,
        mesh=mesh,
        in_specs=placed,
        out_specs=(P("grp", "tp"), P("tp", "grp")),
        check_vma=False,
    )
```

```python
import jax
import jax.numpy as jnp
from jax import lax
from jax.experimental import pallas as pl
from jax.experimental.pallas import tpu as pltpu
from jax.experimental import pallas as pl
from jax.experimental.pallas import tpu as pltpu
from jax.sharding import PartitionSpec as P

HEAD_DIM = 128
QUARTER = 8192


def tp_moves(move):
    return [(chip * 2 + core, move(chip, core)) for chip in range(8) for core in range(2)]


def grp_moves(move):
    return [(z * 2 + plane, move(z, plane)) for z in range(8) for plane in range(2)]


def swap_core(value):
    return lax.ppermute(value, "tp", tp_moves(lambda chip, core: chip * 2 + 1 - core))


def from_z(value, ahead):
    return lax.ppermute(
        value, "grp", grp_moves(lambda z, plane: (z - ahead) % 8 * 2 + plane)
    )


def flip_z(value, k):
    return lax.ppermute(value, "grp", grp_moves(lambda z, plane: (z ^ k) * 2 + plane))


def flip_plane(value):
    return lax.ppermute(value, "grp", grp_moves(lambda z, plane: z * 2 + 1 - plane))


def chip_at(chip, dx, dy):
    return (chip // 4 + dx) % 2 * 4 + (chip + dy) % 4


def to_chip(value, dx, dy):
    return lax.ppermute(
        value, "tp", tp_moves(lambda chip, core: chip_at(chip, dx, dy) * 2 + core)
    )


def attend(queries, kv_cache, new_kv, lengths, kv_index):
    row_count = queries.shape[0]
    own_heads = queries.shape[1] // HEAD_DIM
    slot_count = kv_cache.shape[3]
    score_scale = HEAD_DIM ** (-0.5)
    query_heads = queries.reshape(row_count, own_heads, HEAD_DIM)
    cache_keys = kv_cache[0, :, 0]
    cache_values = kv_cache[1, :, 0]
    new_key = lax.dynamic_index_in_dim(new_kv[0], kv_index, 1, keepdims=False)
    new_value = lax.dynamic_index_in_dim(new_kv[1], kv_index, 1, keepdims=False)
    scores = (
        jnp.einsum("shd,spd->shp", query_heads, cache_keys, preferred_element_type=jnp.float32)
        * score_scale
    )
    new_score = (
        jnp.einsum("shd,sd->sh", query_heads, new_key, preferred_element_type=jnp.float32)
        * score_scale
    )
    slot_index = jnp.arange(slot_count, dtype=jnp.int32)
    is_valid = (slot_index[None, :] < lengths[:, None])[:, None, :]
    top_score = jnp.maximum(jnp.max(jnp.where(is_valid, scores, -jnp.inf), axis=-1), new_score)
    prob_cache = jnp.where(is_valid, jnp.exp(scores - top_score[..., None]), 0.0)
    new_prob = jnp.exp(new_score - top_score)
    total_weight = jnp.sum(prob_cache, axis=-1) + new_prob
    new_rounded = lax.optimization_barrier(new_prob.astype(jnp.bfloat16)).astype(jnp.float32)
    weighted = jnp.einsum(
        "shp,spd->shd",
        prob_cache.astype(jnp.bfloat16),
        cache_values,
        preferred_element_type=jnp.float32,
    )
    weighted = weighted + new_rounded[..., None] * new_value.astype(jnp.float32)[:, None, :]
    return (
        (weighted / total_weight[..., None])
        .astype(jnp.bfloat16)
        .reshape(row_count, own_heads * HEAD_DIM)
    )


def mm(a, b):
    return jnp.dot(a, b, preferred_element_type=jnp.float32)


def project_kernel(core_ref, mine_ref, other_ref, *refs):
    weight_refs, out_ref = refs[:4], refs[4]
    for i in range(2):
        out_ref[i] = (
            mm(mine_ref[...], weight_refs[i][...]) + mm(other_ref[...], weight_refs[2 + i][...])
        ).astype(out_ref.dtype)


def project(core, heads_mine, heads_other, w_mine, w_other, width):
    rows, depth = heads_mine.shape
    columns = [pl.BlockSpec((depth, width), lambda i, core_ref, e=e: (0, 4 * i + 2 * e + core_ref[0])) for e in range(2)]
    whole = pl.BlockSpec((rows, depth), lambda i, core_ref: (0, 0))
    return pl.pallas_call(
        project_kernel,
        grid_spec=pltpu.PrefetchScalarGridSpec(
            num_scalar_prefetch=1,
            grid=(4,),
            in_specs=[whole, whole] + columns + columns,
            out_specs=pl.BlockSpec((2, rows, width), lambda i, core_ref: (i, 0, 0)),
        ),
        out_shape=jax.ShapeDtypeStruct((8, rows, width), jnp.bfloat16),
        cost_estimate=pl.CostEstimate(
            flops=2 * rows * 2 * depth * 8 * width,
            bytes_accessed=2 * 2 * depth * 8 * width,
            transcendentals=0,
        ),
        name="project",
    )(core.reshape(1), heads_mine, heads_other, w_mine, w_mine, w_other, w_other)


def encode_kernel(place_ref, *refs):
    block_refs, (bias_ref, w_mine_ref, w_other_ref) = refs[:8], refs[8:11]
    out_refs, table_ref = refs[11:19], refs[19]
    x_ref, held_ref, row_ref, sems = refs[20:]
    f32 = jnp.float32
    step = pl.program_id(0)
    half, tile = w_mine_ref.shape
    rows = out_refs[0].shape[0]
    lanes = held_ref.shape[1]

    @pl.when(step == 0)
    def _():
        copies = [
            pltpu.make_async_copy(
                block_refs[k],
                x_ref.at[pl.ds(pl.multiple_of(place_ref[k] * rows, rows), rows), :],
                sems.at[k],
            )
            for k in range(8)
        ]
        for copy in copies:
            copy.start()
        held_ref[...] = jnp.zeros_like(held_ref)
        for copy in copies:
            copy.wait()

    part = mm(x_ref[:, :half], w_mine_ref[...]) + mm(x_ref[:, half : 2 * half], w_other_ref[...])
    part = part.astype(jnp.bfloat16)
    for slot in range(8):
        out_refs[slot][...] = part[slot * rows : (slot + 1) * rows]
    first_id = (
        x_ref[:, 2 * half : 2 * half + 1].astype(f32) * 256.0
        + x_ref[:, 2 * half + 1 : 2 * half + 2].astype(f32)
    ).astype(jnp.int32)
    want = (first_id & (QUARTER - 1)) - place_ref[16] - step * tile
    for at in range(0, tile, lanes):
        piece = part[:, at : at + lanes].astype(f32) + bias_ref[:, at : at + lanes]
        column = lax.broadcasted_iota(jnp.int32, piece.shape, 1) + at
        held_ref[...] += jnp.where(column == want, piece, 0.0)

    @pl.when(step == pl.num_programs(0) - 1)
    def _():
        over_lanes = lambda a, b, precision: lax.dot_general(
            a, b, (((1,), (1,)), ((), ())), precision=precision, preferred_element_type=f32
        )
        now = over_lanes(jnp.ones((8, lanes), f32), held_ref[...], lax.Precision.HIGHEST)[:1]
        shape = (16, lanes)
        pick = lax.broadcasted_iota(jnp.int32, shape, 0) == lax.broadcasted_iota(jnp.int32, shape, 1)
        pick = pick.astype(f32).astype(jnp.bfloat16)
        extra = over_lanes(pick, x_ref[:, 2 * half :], None)
        ids = (extra[0:1] * 256.0 + extra[1:2]).astype(jnp.int32)
        local = ((ids & (QUARTER - 1)) - place_ref[16]).astype(f32)
        index = (place_ref[17] - (ids >> 13)) & 3
        value = jnp.zeros_like(local)
        for c in range(4):
            whole = extra[2 + 3 * c : 3 + 3 * c] + extra[3 + 3 * c : 4 + 3 * c]
            value += jnp.where(index == c, whole + extra[4 + 3 * c : 5 + 3 * c], 0.0)
        row_ref[...] = jnp.zeros_like(row_ref)
        for slot in range(8):
            for at, source in enumerate((now, local, value)):
                row_ref[pl.ds(8 * at + place_ref[8 + slot], 1), :rows] = source[
                    :, slot * rows : (slot + 1) * rows
                ]
        for i in range(16):
            table_ref[i] = row_ref[...]


def encode(block, place, bias, w_mine, w_other):
    rows, depth = block[0].shape
    count = 8 * rows
    half, span = w_mine.shape
    tile = 512
    return pl.pallas_call(
        encode_kernel,
        grid_spec=pltpu.PrefetchScalarGridSpec(
            num_scalar_prefetch=1,
            grid=(span // tile,),
            in_specs=[pl.BlockSpec(memory_space=pl.ANY)] * 8
            + [
                pl.BlockSpec((1, tile), lambda i, place: (0, i)),
                pl.BlockSpec((half, tile), lambda i, place: (0, i)),
                pl.BlockSpec((half, tile), lambda i, place: (0, i)),
            ],
            out_specs=[pl.BlockSpec((rows, tile), lambda i, place: (0, i))] * 8
            + [pl.BlockSpec((16, 24, 128), lambda i, place: (0, 0, 0))],
            scratch_shapes=[
                pltpu.VMEM((count, depth), jnp.bfloat16),
                pltpu.VMEM((count, 128), jnp.float32),
                pltpu.VMEM((24, 128), jnp.float32),
                pltpu.SemaphoreType.DMA((8,)),
            ],
        ),
        out_shape=[jax.ShapeDtypeStruct((rows, span), jnp.bfloat16)] * 8
        + [jax.ShapeDtypeStruct((16, 24, 128), jnp.float32)],
        cost_estimate=pl.CostEstimate(
            flops=4 * count * half * span,
            bytes_accessed=2 * (2 * half * span + count * (depth + span)),
            transcendentals=0,
        ),
        name="encode",
    )(place, *block, bias, w_mine, w_other)


def per_device(
    resid_in,
    queries,
    kv_cache,
    new_kv,
    lengths,
    out_weight,
    enc_weight,
    enc_bias,
    dec_weight,
    clamp_ids,
    clamp_values,
):
    f32, bf16 = jnp.float32, jnp.bfloat16
    tp_rank, grp_rank = lax.axis_index("tp"), lax.axis_index("grp")
    chip, core = tp_rank // 2, tp_rank % 2
    z, plane = grp_rank // 2, grp_rank % 2
    rows, width = resid_in.shape
    span = enc_weight.shape[1]
    my_quarter = z // 2

    out_other = swap_core(out_weight)
    enc_other = swap_core(enc_weight)

    heads_mine = attend(queries, kv_cache, new_kv, lengths, tp_rank // 4)
    heads_other = swap_core(heads_mine)
    part = project(core, heads_mine, heads_other, out_weight, out_other, width)
    groups = [[c + 2 * i for i in range(8)] for c in range(2)]
    arrived = lax.all_to_all(part, "tp", 0, 0, axis_index_groups=groups, tiled=True)
    resid_mid = (resid_in.astype(f32) + jnp.sum(arrived.astype(f32), axis=0)).astype(bf16)

    mid_other = swap_core(resid_mid)
    coarse = lambda value: lax.reduce_precision(value, 8, 7)
    high = coarse(clamp_values)
    middle = coarse(clamp_values - high)
    parts = jnp.stack([high, middle, clamp_values - high - middle], axis=2).reshape(rows, 12)
    first_id = clamp_ids[:, :1]
    id_parts = jnp.concatenate([first_id // 256, first_id % 256], axis=1).astype(f32)
    extra = jnp.concatenate([id_parts, parts, jnp.zeros((rows, 114), f32)], axis=1).astype(bf16)
    both = jnp.concatenate([resid_mid, mid_other, extra], axis=1)
    cross = [
        (t * 16 + z_ * 2 + t % 2, t * 16 + z_ * 2 + 1 - t % 2) for t in range(16) for z_ in range(8)
    ]
    crossed = lax.ppermute(both, ("tp", "grp"), cross)
    block = [None] * 8
    block[0] = jnp.where(core == plane, both, crossed)
    for k, source, step in (
        (1, 0, 1), (7, 0, 7), (2, 0, 2), (6, 0, 6),
        (3, 2, 1), (5, 6, 7), (4, 2, 2),
    ):
        block[k] = from_z(block[source], step)
    ahead = (jnp.arange(8, dtype=jnp.int32) + z) % 8
    slot = (ahead // 4 + chip // 4) % 2 * 4 + (ahead - chip) % 4
    bias = jnp.where(chip == 0, enc_bias, 0.0).reshape(1, span)
    each = jnp.arange(8, dtype=jnp.int32)
    goal = ((chip // 4 + each // 4) % 2 * 4 + (chip + each) % 4 - z) % 8
    others = jnp.stack([grp_rank % 4 * span, my_quarter])
    outs = encode(
        block, jnp.concatenate([slot, goal, others]), bias, enc_weight, enc_other
    )

    table = lax.all_to_all(outs[8], "tp", 0, 0, tiled=True)
    table = table[:, :, :rows].reshape(8, 2, 24, rows)
    now = jnp.maximum(table[:, :, :8].sum(axis=0), 0.0)
    now = lax.reduce_precision(now, 8, 7)
    want, delta = table[0, :, 8:16], table[0, :, 16:] - now

    def arrange(value):
        value = jnp.where(plane == 1, value, value[::-1])
        odd = value[:, 1::2]
        odd = jnp.where(z % 2 == 0, odd, jnp.concatenate([odd[:, 3:], odd[:, :3]], axis=1))
        return odd.reshape(8 * rows), value[:, 0::2].reshape(8 * rows)

    def decode(want, delta):
        column = jnp.arange(span, dtype=jnp.int32)[None, :]
        hits = jnp.where(column == want.astype(jnp.int32)[:, None], delta[:, None], 0.0)
        return mm(hits.astype(bf16), dec_weight)

    want_give, want_keep = arrange(want)
    delta_give, delta_keep = arrange(delta)
    give = decode(want_give, delta_give).astype(bf16)
    near = flip_z(give, 1)
    keep = decode(want_keep, delta_keep).astype(bf16)
    first, last = slice(0, 4 * rows), slice(4 * rows, 8 * rows)
    near_2 = flip_plane(keep[first] + near[first])
    found = keep[last] + near[last] + near_2
    edit = found[:rows].astype(f32)
    edits = []
    for k in (1, 2, 3):
        edits.append(from_z(found[k * rows : (k + 1) * rows], -2 * k))

    relayed = to_chip(outs[6], 0, 3)
    seven = outs[7] + relayed
    relayed = to_chip(outs[2], 0, 1)
    one = outs[1] + relayed
    moved = []
    for value, s in ((outs[4], 4), (outs[5], 5), (outs[3], 3), (seven, 7), (one, 1)):
        moved.append(to_chip(value, s // 4, s % 4))

    total = outs[0].astype(f32)
    for value in moved:
        total = total + value.astype(f32)
    features = jnp.maximum(total + enc_bias, 0.0).astype(bf16)

    for value in edits:
        edit = edit + value.astype(f32)
    resid_out = (resid_mid.astype(f32) + edit).astype(bf16)
    return (resid_out, features)


def solution(mesh):
    placed = (
        P("grp", "tp"),
        P("grp", "tp"),
        P(None, "grp", "tp", None, None),
        P(None, "grp", None, None),
        P("grp"),
        P("tp", None),
        P("tp", "grp"),
        P("grp"),
        P("grp", "tp"),
        P("grp", None),
        P("grp", None),
    )
    return jax.shard_map(
        per_device,
        mesh=mesh,
        in_specs=placed,
        out_specs=(P("grp", "tp"), P("tp", "grp")),
        check_vma=False,
    )
```

```python
import jax
import jax.numpy as jnp
from jax import lax
from jax.experimental import pallas as pl
from jax.experimental.pallas import tpu as pltpu
from jax.experimental import pallas as pl
from jax.experimental.pallas import tpu as pltpu
from jax.sharding import PartitionSpec as P

HEAD_DIM = 128
QUARTER = 8192


def tp_moves(move):
    return [(chip * 2 + core, move(chip, core)) for chip in range(8) for core in range(2)]


def grp_moves(move):
    return [(z * 2 + plane, move(z, plane)) for z in range(8) for plane in range(2)]


def swap_core(value):
    return lax.ppermute(value, "tp", tp_moves(lambda chip, core: chip * 2 + 1 - core))


def from_z(value, ahead):
    return lax.ppermute(
        value, "grp", grp_moves(lambda z, plane: (z - ahead) % 8 * 2 + plane)
    )


def flip_z(value, k):
    return lax.ppermute(value, "grp", grp_moves(lambda z, plane: (z ^ k) * 2 + plane))


def flip_plane(value):
    return lax.ppermute(value, "grp", grp_moves(lambda z, plane: z * 2 + 1 - plane))


def chip_at(chip, dx, dy):
    return (chip // 4 + dx) % 2 * 4 + (chip + dy) % 4


def to_chip(value, dx, dy):
    return lax.ppermute(
        value, "tp", tp_moves(lambda chip, core: chip_at(chip, dx, dy) * 2 + core)
    )


def attend(queries, kv_cache, new_kv, lengths, kv_index):
    row_count = queries.shape[0]
    own_heads = queries.shape[1] // HEAD_DIM
    slot_count = kv_cache.shape[3]
    score_scale = HEAD_DIM ** (-0.5)
    query_heads = queries.reshape(row_count, own_heads, HEAD_DIM)
    cache_keys = kv_cache[0, :, 0]
    cache_values = kv_cache[1, :, 0]
    new_key = lax.dynamic_index_in_dim(new_kv[0], kv_index, 1, keepdims=False)
    new_value = lax.dynamic_index_in_dim(new_kv[1], kv_index, 1, keepdims=False)
    scores = (
        jnp.einsum("shd,spd->shp", query_heads, cache_keys, preferred_element_type=jnp.float32)
        * score_scale
    )
    new_score = (
        jnp.einsum("shd,sd->sh", query_heads, new_key, preferred_element_type=jnp.float32)
        * score_scale
    )
    slot_index = jnp.arange(slot_count, dtype=jnp.int32)
    is_valid = (slot_index[None, :] < lengths[:, None])[:, None, :]
    top_score = jnp.maximum(jnp.max(jnp.where(is_valid, scores, -jnp.inf), axis=-1), new_score)
    prob_cache = jnp.where(is_valid, jnp.exp(scores - top_score[..., None]), 0.0)
    new_prob = jnp.exp(new_score - top_score)
    total_weight = jnp.sum(prob_cache, axis=-1) + new_prob
    new_rounded = lax.optimization_barrier(new_prob.astype(jnp.bfloat16)).astype(jnp.float32)
    weighted = jnp.einsum(
        "shp,spd->shd",
        prob_cache.astype(jnp.bfloat16),
        cache_values,
        preferred_element_type=jnp.float32,
    )
    weighted = weighted + new_rounded[..., None] * new_value.astype(jnp.float32)[:, None, :]
    return (
        (weighted / total_weight[..., None])
        .astype(jnp.bfloat16)
        .reshape(row_count, own_heads * HEAD_DIM)
    )


def mm(a, b):
    return jnp.dot(a, b, preferred_element_type=jnp.float32)


def project_kernel(core_ref, mine_ref, other_ref, *refs):
    weight_refs, out_ref = refs[:4], refs[4]
    for i in range(2):
        out_ref[i] = (
            mm(mine_ref[...], weight_refs[i][...]) + mm(other_ref[...], weight_refs[2 + i][...])
        ).astype(out_ref.dtype)


def project(core, heads_mine, heads_other, w_mine, w_other, width):
    rows, depth = heads_mine.shape
    columns = [pl.BlockSpec((depth, width), lambda i, core_ref, e=e: (0, 4 * i + 2 * e + core_ref[0])) for e in range(2)]
    whole = pl.BlockSpec((rows, depth), lambda i, core_ref: (0, 0))
    return pl.pallas_call(
        project_kernel,
        grid_spec=pltpu.PrefetchScalarGridSpec(
            num_scalar_prefetch=1,
            grid=(4,),
            in_specs=[whole, whole] + columns + columns,
            out_specs=pl.BlockSpec((2, rows, width), lambda i, core_ref: (i, 0, 0)),
        ),
        out_shape=jax.ShapeDtypeStruct((8, rows, width), jnp.bfloat16),
        cost_estimate=pl.CostEstimate(
            flops=2 * rows * 2 * depth * 8 * width,
            bytes_accessed=2 * 2 * depth * 8 * width,
            transcendentals=0,
        ),
        name="project",
    )(core.reshape(1), heads_mine, heads_other, w_mine, w_mine, w_other, w_other)


def encode_kernel(place_ref, *refs):
    block_refs, (bias_ref, w_mine_ref, w_other_ref) = refs[:8], refs[8:11]
    out_refs, table_ref = refs[11:19], refs[19]
    x_ref, held_ref, row_ref, sems = refs[20:]
    f32 = jnp.float32
    step = pl.program_id(0)
    half, tile = w_mine_ref.shape
    rows = out_refs[0].shape[0]
    lanes = held_ref.shape[1]

    @pl.when(step == 0)
    def _():
        copies = [
            pltpu.make_async_copy(
                block_refs[k],
                x_ref.at[pl.ds(pl.multiple_of(place_ref[k] * rows, rows), rows), :],
                sems.at[k],
            )
            for k in range(8)
        ]
        for copy in copies:
            copy.start()
        held_ref[...] = jnp.zeros_like(held_ref)
        for copy in copies:
            copy.wait()

    part = mm(x_ref[:, :half], w_mine_ref[...]) + mm(x_ref[:, half : 2 * half], w_other_ref[...])
    part = part.astype(jnp.bfloat16)
    for slot in range(8):
        out_refs[slot][...] = part[slot * rows : (slot + 1) * rows]
    first_id = (
        x_ref[:, 2 * half : 2 * half + 1].astype(f32) * 256.0
        + x_ref[:, 2 * half + 1 : 2 * half + 2].astype(f32)
    ).astype(jnp.int32)
    want = (first_id & (QUARTER - 1)) - place_ref[16] - step * tile
    for at in range(0, tile, lanes):
        piece = part[:, at : at + lanes].astype(f32) + bias_ref[:, at : at + lanes]
        column = lax.broadcasted_iota(jnp.int32, piece.shape, 1) + at
        held_ref[...] += jnp.where(column == want, piece, 0.0)

    @pl.when(step == pl.num_programs(0) - 1)
    def _():
        over_lanes = lambda a, b, precision: lax.dot_general(
            a, b, (((1,), (1,)), ((), ())), precision=precision, preferred_element_type=f32
        )
        now = over_lanes(jnp.ones((8, lanes), f32), held_ref[...], lax.Precision.HIGHEST)[:1]
        shape = (16, lanes)
        pick = lax.broadcasted_iota(jnp.int32, shape, 0) == lax.broadcasted_iota(jnp.int32, shape, 1)
        pick = pick.astype(f32).astype(jnp.bfloat16)
        extra = over_lanes(pick, x_ref[:, 2 * half :], None)
        ids = (extra[0:1] * 256.0 + extra[1:2]).astype(jnp.int32)
        local = ((ids & (QUARTER - 1)) - place_ref[16]).astype(f32)
        index = (place_ref[17] - (ids >> 13)) & 3
        value = jnp.zeros_like(local)
        for c in range(4):
            whole = extra[2 + 3 * c : 3 + 3 * c] + extra[3 + 3 * c : 4 + 3 * c]
            value += jnp.where(index == c, whole + extra[4 + 3 * c : 5 + 3 * c], 0.0)
        row_ref[...] = jnp.zeros_like(row_ref)
        for slot in range(8):
            for at, source in enumerate((now, local, value)):
                row_ref[pl.ds(8 * at + place_ref[8 + slot], 1), :rows] = source[
                    :, slot * rows : (slot + 1) * rows
                ]
        for i in range(16):
            table_ref[i] = row_ref[...]


def encode(block, place, bias, w_mine, w_other):
    rows, depth = block[0].shape
    count = 8 * rows
    half, span = w_mine.shape
    tile = 512
    return pl.pallas_call(
        encode_kernel,
        grid_spec=pltpu.PrefetchScalarGridSpec(
            num_scalar_prefetch=1,
            grid=(span // tile,),
            in_specs=[pl.BlockSpec(memory_space=pl.ANY)] * 8
            + [
                pl.BlockSpec((1, tile), lambda i, place: (0, i)),
                pl.BlockSpec((half, tile), lambda i, place: (0, i)),
                pl.BlockSpec((half, tile), lambda i, place: (0, i)),
            ],
            out_specs=[pl.BlockSpec((rows, tile), lambda i, place: (0, i))] * 8
            + [pl.BlockSpec((16, 24, 128), lambda i, place: (0, 0, 0))],
            scratch_shapes=[
                pltpu.VMEM((count, depth), jnp.bfloat16),
                pltpu.VMEM((count, 128), jnp.float32),
                pltpu.VMEM((24, 128), jnp.float32),
                pltpu.SemaphoreType.DMA((8,)),
            ],
        ),
        out_shape=[jax.ShapeDtypeStruct((rows, span), jnp.bfloat16)] * 8
        + [jax.ShapeDtypeStruct((16, 24, 128), jnp.float32)],
        cost_estimate=pl.CostEstimate(
            flops=4 * count * half * span,
            bytes_accessed=2 * (2 * half * span + count * (depth + span)),
            transcendentals=0,
        ),
        name="encode",
    )(place, *block, bias, w_mine, w_other)


def per_device(
    resid_in,
    queries,
    kv_cache,
    new_kv,
    lengths,
    out_weight,
    enc_weight,
    enc_bias,
    dec_weight,
    clamp_ids,
    clamp_values,
):
    f32, bf16 = jnp.float32, jnp.bfloat16
    tp_rank, grp_rank = lax.axis_index("tp"), lax.axis_index("grp")
    chip, core = tp_rank // 2, tp_rank % 2
    z, plane = grp_rank // 2, grp_rank % 2
    rows, width = resid_in.shape
    span = enc_weight.shape[1]
    my_quarter = z // 2

    out_other = swap_core(out_weight)
    enc_other = swap_core(enc_weight)

    heads_mine = attend(queries, kv_cache, new_kv, lengths, tp_rank // 4)
    heads_other = swap_core(heads_mine)
    part = project(core, heads_mine, heads_other, out_weight, out_other, width)
    groups = [[c + 2 * i for i in range(8)] for c in range(2)]
    arrived = lax.all_to_all(part, "tp", 0, 0, axis_index_groups=groups, tiled=True)
    resid_mid = (resid_in.astype(f32) + jnp.sum(arrived.astype(f32), axis=0)).astype(bf16)

    mid_other = swap_core(resid_mid)
    coarse = lambda value: lax.reduce_precision(value, 8, 7)
    high = coarse(clamp_values)
    middle = coarse(clamp_values - high)
    parts = jnp.stack([high, middle, clamp_values - high - middle], axis=2).reshape(rows, 12)
    first_id = clamp_ids[:, :1]
    id_parts = jnp.concatenate([first_id // 256, first_id % 256], axis=1).astype(f32)
    extra = jnp.concatenate([id_parts, parts, jnp.zeros((rows, 114), f32)], axis=1).astype(bf16)
    both = jnp.concatenate([resid_mid, mid_other, extra], axis=1)
    cross = [
        (t * 16 + z_ * 2 + t % 2, t * 16 + z_ * 2 + 1 - t % 2) for t in range(16) for z_ in range(8)
    ]
    crossed = lax.ppermute(both, ("tp", "grp"), cross)
    block = [None] * 8
    block[0] = jnp.where(core == plane, both, crossed)
    for k, source, step in (
        (1, 0, 1), (7, 0, 7), (2, 0, 2), (6, 0, 6),
        (3, 2, 1), (5, 6, 7), (4, 2, 2),
    ):
        block[k] = from_z(block[source], step)
    ahead = (jnp.arange(8, dtype=jnp.int32) + z) % 8
    slot = (ahead // 4 + chip // 4) % 2 * 4 + (ahead - chip) % 4
    bias = jnp.where(chip == 0, enc_bias, 0.0).reshape(1, span)
    each = jnp.arange(8, dtype=jnp.int32)
    goal = ((chip // 4 + each // 4) % 2 * 4 + (chip + each) % 4 - z) % 8
    others = jnp.stack([grp_rank % 4 * span, my_quarter])
    outs = encode(
        block, jnp.concatenate([slot, goal, others]), bias, enc_weight, enc_other
    )

    table = lax.all_to_all(outs[8], "tp", 0, 0, tiled=True)
    table = table[:, :, :rows].reshape(8, 2, 24, rows)
    now = jnp.maximum(table[:, :, :8].sum(axis=0), 0.0)
    now = lax.reduce_precision(now, 8, 7)
    want, delta = table[0, :, 8:16], table[0, :, 16:] - now

    even_z = z % 2 == 0
    half = width // 2

    def arrange(value):
        value = jnp.where(plane == 1, value, value[::-1])
        odd = value[:, 1::2]
        turned = jnp.concatenate([odd[:, 3:], odd[:, :3]], axis=1)
        parts = jnp.where(even_z, odd, turned), jnp.where(even_z, turned, odd), value[:, 0::2]
        return [part.reshape(8 * rows) for part in parts]

    def decode(want, delta, weight):
        column = jnp.arange(span, dtype=jnp.int32)[None, :]
        hits = jnp.where(column == want.astype(jnp.int32)[:, None], delta[:, None], 0.0)
        return mm(hits.astype(bf16), weight).astype(bf16)

    wants, deltas = arrange(want), arrange(delta)
    give = decode(wants[0], deltas[0], dec_weight[:, :half])
    near_left = flip_z(give, 1)
    give = decode(wants[1], deltas[1], dec_weight[:, half:])
    near_right = lax.ppermute(
        give, "grp", grp_moves(lambda z_, s: (z_ + (7 if z_ % 2 == 0 else 1)) % 8 * 2 + s)
    )
    keep = decode(wants[2], deltas[2], dec_weight)
    first, last = slice(0, 4 * rows), slice(4 * rows, 8 * rows)
    near = jnp.concatenate([near_left, near_right], axis=1)
    near_2 = flip_plane(keep[first] + near[first])
    found = keep[last] + near[last] + near_2
    edit = found[:rows].astype(f32)
    edits = []
    for k in (1, 2, 3):
        edits.append(from_z(found[k * rows : (k + 1) * rows], -2 * k))

    relayed = to_chip(outs[6], 0, 3)
    seven = outs[7] + relayed
    relayed = to_chip(outs[2], 0, 1)
    one = outs[1] + relayed
    moved = []
    for value, s in ((outs[4], 4), (outs[5], 5), (outs[3], 3), (seven, 7), (one, 1)):
        moved.append(to_chip(value, s // 4, s % 4))

    total = outs[0].astype(f32)
    for value in moved:
        total = total + value.astype(f32)
    features = jnp.maximum(total + enc_bias, 0.0).astype(bf16)

    for value in edits:
        edit = edit + value.astype(f32)
    resid_out = (resid_mid.astype(f32) + edit).astype(bf16)
    return (resid_out, features)


def solution(mesh):
    placed = (
        P("grp", "tp"),
        P("grp", "tp"),
        P(None, "grp", "tp", None, None),
        P(None, "grp", None, None),
        P("grp"),
        P("tp", None),
        P("tp", "grp"),
        P("grp"),
        P("grp", "tp"),
        P("grp", None),
        P("grp", None),
    )
    return jax.shard_map(
        per_device,
        mesh=mesh,
        in_specs=placed,
        out_specs=(P("grp", "tp"), P("tp", "grp")),
        check_vma=False,
    )
```

```python
import jax
import jax.numpy as jnp
from jax import lax
from jax.experimental import pallas as pl
from jax.experimental.pallas import tpu as pltpu
from jax.experimental import pallas as pl
from jax.experimental.pallas import tpu as pltpu
from jax.sharding import PartitionSpec as P

HEAD_DIM = 128
QUARTER = 8192


def tp_moves(move):
    return [(chip * 2 + core, move(chip, core)) for chip in range(8) for core in range(2)]


def grp_moves(move):
    return [(z * 2 + plane, move(z, plane)) for z in range(8) for plane in range(2)]


def swap_core(value):
    return lax.ppermute(value, "tp", tp_moves(lambda chip, core: chip * 2 + 1 - core))


def from_z(value, ahead):
    return lax.ppermute(
        value, "grp", grp_moves(lambda z, plane: (z - ahead) % 8 * 2 + plane)
    )


def flip_z(value, k):
    return lax.ppermute(value, "grp", grp_moves(lambda z, plane: (z ^ k) * 2 + plane))


def flip_plane(value):
    return lax.ppermute(value, "grp", grp_moves(lambda z, plane: z * 2 + 1 - plane))


def chip_at(chip, dx, dy):
    return (chip // 4 + dx) % 2 * 4 + (chip + dy) % 4


def to_chip(value, dx, dy):
    return lax.ppermute(
        value, "tp", tp_moves(lambda chip, core: chip_at(chip, dx, dy) * 2 + core)
    )


def attend(queries, kv_cache, new_kv, lengths, kv_index):
    row_count = queries.shape[0]
    own_heads = queries.shape[1] // HEAD_DIM
    slot_count = kv_cache.shape[3]
    score_scale = HEAD_DIM ** (-0.5)
    query_heads = queries.reshape(row_count, own_heads, HEAD_DIM)
    cache_keys = kv_cache[0, :, 0]
    cache_values = kv_cache[1, :, 0]
    chosen = lax.dynamic_index_in_dim(new_kv, kv_index, 2, keepdims=False)
    new_key, new_value = chosen[0], chosen[1]
    scores = (
        jnp.einsum("shd,spd->shp", query_heads, cache_keys, preferred_element_type=jnp.float32)
        * score_scale
    )
    new_score = (
        jnp.einsum("shd,sd->sh", query_heads, new_key, preferred_element_type=jnp.float32)
        * score_scale
    )
    slot_index = jnp.arange(slot_count, dtype=jnp.int32)
    is_valid = (slot_index[None, :] < lengths[:, None])[:, None, :]
    top_score = jnp.maximum(jnp.max(jnp.where(is_valid, scores, -jnp.inf), axis=-1), new_score)
    prob_cache = jnp.where(is_valid, jnp.exp(scores - top_score[..., None]), 0.0)
    new_prob = jnp.exp(new_score - top_score)
    total_weight = jnp.sum(prob_cache, axis=-1) + new_prob
    new_rounded = lax.optimization_barrier(new_prob.astype(jnp.bfloat16)).astype(jnp.float32)
    weighted = jnp.einsum(
        "shp,spd->shd",
        prob_cache.astype(jnp.bfloat16),
        cache_values,
        preferred_element_type=jnp.float32,
    )
    weighted = weighted + new_rounded[..., None] * new_value.astype(jnp.float32)[:, None, :]
    return (
        (weighted / total_weight[..., None])
        .astype(jnp.bfloat16)
        .reshape(row_count, own_heads * HEAD_DIM)
    )


def mm(a, b):
    return jnp.dot(a, b, preferred_element_type=jnp.float32)


def project_kernel(core_ref, mine_ref, other_ref, *refs):
    weight_refs, out_ref = refs[:4], refs[4]
    for i in range(2):
        out_ref[i] = (
            mm(mine_ref[...], weight_refs[i][...]) + mm(other_ref[...], weight_refs[2 + i][...])
        ).astype(out_ref.dtype)


def project(core, heads_mine, heads_other, w_mine, w_other, width):
    rows, depth = heads_mine.shape
    columns = [pl.BlockSpec((depth, width), lambda i, core_ref, e=e: (0, 4 * i + 2 * e + core_ref[0])) for e in range(2)]
    whole = pl.BlockSpec((rows, depth), lambda i, core_ref: (0, 0))
    return pl.pallas_call(
        project_kernel,
        grid_spec=pltpu.PrefetchScalarGridSpec(
            num_scalar_prefetch=1,
            grid=(4,),
            in_specs=[whole, whole] + columns + columns,
            out_specs=pl.BlockSpec((2, rows, width), lambda i, core_ref: (i, 0, 0)),
        ),
        out_shape=jax.ShapeDtypeStruct((8, rows, width), jnp.bfloat16),
        cost_estimate=pl.CostEstimate(
            flops=2 * rows * 2 * depth * 8 * width,
            bytes_accessed=2 * 2 * depth * 8 * width,
            transcendentals=0,
        ),
        name="project",
    )(core.reshape(1), heads_mine, heads_other, w_mine, w_mine, w_other, w_other)


def encode_kernel(place_ref, *refs):
    block_refs, (bias_ref, w_mine_ref, w_other_ref) = refs[:8], refs[8:11]
    out_refs, table_ref = refs[11:19], refs[19]
    x_ref, held_ref, row_ref, sems = refs[20:]
    f32 = jnp.float32
    step = pl.program_id(0)
    half, tile = w_mine_ref.shape
    rows = out_refs[0].shape[0]
    lanes = held_ref.shape[1]

    @pl.when(step == 0)
    def _():
        copies = [
            pltpu.make_async_copy(
                block_refs[k],
                x_ref.at[pl.ds(pl.multiple_of(place_ref[k] * rows, rows), rows), :],
                sems.at[k],
            )
            for k in range(8)
        ]
        for copy in copies:
            copy.start()
        held_ref[...] = jnp.zeros_like(held_ref)
        for copy in copies:
            copy.wait()

    part = mm(x_ref[:, :half], w_mine_ref[...]) + mm(x_ref[:, half : 2 * half], w_other_ref[...])
    part = part.astype(jnp.bfloat16)
    for slot in range(8):
        out_refs[slot][...] = part[slot * rows : (slot + 1) * rows]
    first_id = (
        x_ref[:, 2 * half : 2 * half + 1].astype(f32) * 256.0
        + x_ref[:, 2 * half + 1 : 2 * half + 2].astype(f32)
    ).astype(jnp.int32)
    want = (first_id & (QUARTER - 1)) - place_ref[16] - step * tile
    for at in range(0, tile, lanes):
        piece = part[:, at : at + lanes].astype(f32) + bias_ref[:, at : at + lanes]
        column = lax.broadcasted_iota(jnp.int32, piece.shape, 1) + at
        held_ref[...] += jnp.where(column == want, piece, 0.0)

    @pl.when(step == pl.num_programs(0) - 1)
    def _():
        over_lanes = lambda a, b, precision: lax.dot_general(
            a, b, (((1,), (1,)), ((), ())), precision=precision, preferred_element_type=f32
        )
        now = over_lanes(jnp.ones((8, lanes), f32), held_ref[...], lax.Precision.HIGHEST)[:1]
        shape = (16, lanes)
        pick = lax.broadcasted_iota(jnp.int32, shape, 0) == lax.broadcasted_iota(jnp.int32, shape, 1)
        pick = pick.astype(f32).astype(jnp.bfloat16)
        extra = over_lanes(pick, x_ref[:, 2 * half :], None)
        ids = (extra[0:1] * 256.0 + extra[1:2]).astype(jnp.int32)
        local = ((ids & (QUARTER - 1)) - place_ref[16]).astype(f32)
        index = (place_ref[17] - (ids >> 13)) & 3
        value = jnp.zeros_like(local)
        for c in range(4):
            whole = extra[2 + 3 * c : 3 + 3 * c] + extra[3 + 3 * c : 4 + 3 * c]
            value += jnp.where(index == c, whole + extra[4 + 3 * c : 5 + 3 * c], 0.0)
        row_ref[...] = jnp.zeros_like(row_ref)
        for slot in range(8):
            for at, source in enumerate((now, local, value)):
                row_ref[pl.ds(8 * at + place_ref[8 + slot], 1), :rows] = source[
                    :, slot * rows : (slot + 1) * rows
                ]
        for i in range(16):
            table_ref[i] = row_ref[...]


def encode(block, place, bias, w_mine, w_other):
    rows, depth = block[0].shape
    count = 8 * rows
    half, span = w_mine.shape
    tile = 1024
    return pl.pallas_call(
        encode_kernel,
        grid_spec=pltpu.PrefetchScalarGridSpec(
            num_scalar_prefetch=1,
            grid=(span // tile,),
            in_specs=[pl.BlockSpec(memory_space=pl.ANY)] * 8
            + [
                pl.BlockSpec((1, tile), lambda i, place: (0, i)),
                pl.BlockSpec((half, tile), lambda i, place: (0, i)),
                pl.BlockSpec((half, tile), lambda i, place: (0, i)),
            ],
            out_specs=[pl.BlockSpec((rows, tile), lambda i, place: (0, i))] * 8
            + [pl.BlockSpec((16, 24, 128), lambda i, place: (0, 0, 0))],
            scratch_shapes=[
                pltpu.VMEM((count, depth), jnp.bfloat16),
                pltpu.VMEM((count, 128), jnp.float32),
                pltpu.VMEM((24, 128), jnp.float32),
                pltpu.SemaphoreType.DMA((8,)),
            ],
        ),
        out_shape=[jax.ShapeDtypeStruct((rows, span), jnp.bfloat16)] * 8
        + [jax.ShapeDtypeStruct((16, 24, 128), jnp.float32)],
        cost_estimate=pl.CostEstimate(
            flops=4 * count * half * span,
            bytes_accessed=2 * (2 * half * span + count * (depth + span)),
            transcendentals=0,
        ),
        name="encode",
    )(place, *block, bias, w_mine, w_other)


def per_device(
    resid_in,
    queries,
    kv_cache,
    new_kv,
    lengths,
    out_weight,
    enc_weight,
    enc_bias,
    dec_weight,
    clamp_ids,
    clamp_values,
):
    f32, bf16 = jnp.float32, jnp.bfloat16
    tp_rank, grp_rank = lax.axis_index("tp"), lax.axis_index("grp")
    chip, core = tp_rank // 2, tp_rank % 2
    z, plane = grp_rank // 2, grp_rank % 2
    rows, width = resid_in.shape
    span = enc_weight.shape[1]
    my_quarter = z // 2

    out_other = swap_core(out_weight)
    enc_other = swap_core(enc_weight)

    heads_mine = attend(queries, kv_cache, new_kv, lengths, tp_rank // 4)
    heads_other = swap_core(heads_mine)
    part = project(core, heads_mine, heads_other, out_weight, out_other, width)
    groups = [[c + 2 * i for i in range(8)] for c in range(2)]
    arrived = lax.all_to_all(part, "tp", 0, 0, axis_index_groups=groups, tiled=True)
    resid_mid = (resid_in.astype(f32) + jnp.sum(arrived.astype(f32), axis=0)).astype(bf16)

    mid_other = swap_core(resid_mid)
    coarse = lambda value: lax.reduce_precision(value, 8, 7)
    high = coarse(clamp_values)
    middle = coarse(clamp_values - high)
    parts = jnp.stack([high, middle, clamp_values - high - middle], axis=2).reshape(rows, 12)
    first_id = clamp_ids[:, :1]
    id_parts = jnp.concatenate([first_id // 256, first_id % 256], axis=1).astype(f32)
    extra = jnp.concatenate([id_parts, parts, jnp.zeros((rows, 114), f32)], axis=1).astype(bf16)
    both = jnp.concatenate([resid_mid, mid_other, extra], axis=1)
    cross = [
        (t * 16 + z_ * 2 + t % 2, t * 16 + z_ * 2 + 1 - t % 2) for t in range(16) for z_ in range(8)
    ]
    crossed = lax.ppermute(both, ("tp", "grp"), cross)
    block = [None] * 8
    block[0] = jnp.where(core == plane, both, crossed)
    for k, source, step in (
        (1, 0, 1), (7, 0, 7), (2, 0, 2), (6, 0, 6),
        (3, 2, 1), (5, 6, 7), (4, 2, 2),
    ):
        block[k] = from_z(block[source], step)
    ahead = (jnp.arange(8, dtype=jnp.int32) + z) % 8
    slot = (ahead // 4 + chip // 4) % 2 * 4 + (ahead - chip) % 4
    bias = jnp.where(chip == 0, enc_bias, 0.0).reshape(1, span)
    each = jnp.arange(8, dtype=jnp.int32)
    goal = ((chip // 4 + each // 4) % 2 * 4 + (chip + each) % 4 - z) % 8
    others = jnp.stack([grp_rank % 4 * span, my_quarter])
    outs = encode(
        block, jnp.concatenate([slot, goal, others]), bias, enc_weight, enc_other
    )

    table = lax.all_to_all(outs[8], "tp", 0, 0, tiled=True)
    table = table[:, :, :rows].reshape(8, 2, 24, rows)
    now = jnp.maximum(table[:, :, :8].sum(axis=0), 0.0)
    now = lax.reduce_precision(now, 8, 7)
    want, delta = table[0, :, 8:16], table[0, :, 16:] - now

    even_z = z % 2 == 0
    half = width // 2

    def arrange(value):
        value = jnp.where(plane == 1, value, value[::-1])
        odd = value[:, 1::2]
        turned = jnp.concatenate([odd[:, 3:], odd[:, :3]], axis=1)
        parts = jnp.where(even_z, odd, turned), jnp.where(even_z, turned, odd), value[:, 0::2]
        return [part.reshape(8 * rows) for part in parts]

    def decode(want, delta, weight):
        column = jnp.arange(span, dtype=jnp.int32)[None, :]
        hits = jnp.where(column == want.astype(jnp.int32)[:, None], delta[:, None], 0.0)
        return mm(hits.astype(bf16), weight).astype(bf16)

    wants, deltas = arrange(want), arrange(delta)
    give = decode(wants[0], deltas[0], dec_weight[:, :half])
    near_left = flip_z(give, 1)
    give = decode(wants[1], deltas[1], dec_weight[:, half:])
    near_right = lax.ppermute(
        give, "grp", grp_moves(lambda z_, s: (z_ + (7 if z_ % 2 == 0 else 1)) % 8 * 2 + s)
    )
    keep = decode(wants[2], deltas[2], dec_weight)
    first, last = slice(0, 4 * rows), slice(4 * rows, 8 * rows)
    near = jnp.concatenate([near_left, near_right], axis=1)
    near_2 = flip_plane(keep[first] + near[first])
    found = keep[last] + near[last] + near_2
    edit = found[:rows].astype(f32)
    edits = []
    for k in (1, 2, 3):
        edits.append(from_z(found[k * rows : (k + 1) * rows], -2 * k))

    relayed = to_chip(outs[6], 0, 3)
    seven = outs[7] + relayed
    relayed = to_chip(outs[2], 0, 1)
    one = outs[1] + relayed
    five = to_chip(outs[5], 0, 1)
    seven = to_chip(seven, 0, 3)
    three = to_chip(outs[3], 0, 3)
    one = to_chip(one, 0, 1)
    four = (outs[4].astype(f32) + five.astype(f32) + seven.astype(f32)).astype(bf16)
    four = to_chip(four, 1, 0)
    moved = [one, three, four]

    total = outs[0].astype(f32)
    for value in moved:
        total = total + value.astype(f32)
    features = jnp.maximum(total + enc_bias, 0.0).astype(bf16)

    for value in edits:
        edit = edit + value.astype(f32)
    resid_out = (resid_mid.astype(f32) + edit).astype(bf16)
    return (resid_out, features)


def solution(mesh):
    placed = (
        P("grp", "tp"),
        P("grp", "tp"),
        P(None, "grp", "tp", None, None),
        P(None, "grp", None, None),
        P("grp"),
        P("tp", None),
        P("tp", "grp"),
        P("grp"),
        P("grp", "tp"),
        P("grp", None),
        P("grp", None),
    )
    return jax.shard_map(
        per_device,
        mesh=mesh,
        in_specs=placed,
        out_specs=(P("grp", "tp"), P("tp", "grp")),
        check_vma=False,
    )
```
